32 devices in a mesh: seq: 8 (over z, x), fsdp: 4 (over y, core).
Axes of the slice: x: 2, y: 2, z: 4, core: 2. Of those that a mesh axis runs over, the one named last changes fastest.
Arguments:
- hidden: bfloat16 [4, 2048, 1536], P('fsdp', 'seq'), may hold values from -6 to 6
- cotangent: bfloat16 [4, 2048, 1536], P('fsdp', 'seq'), may hold values from -6 to 6
- norm_gain: bfloat16 [1536], P('fsdp'), may hold values from 0.5 to 1.5
- in_weight: bfloat16 [1536, 6448], P('fsdp'), may hold values from -0.15625 to 0.15625
- conv_weight: bfloat16 [3328, 4], P('fsdp'), may hold values from -3 to 3
- conv_bias: bfloat16 [3328], P('fsdp'), may hold values from -3 to 3
- dt_bias: bfloat16 [48], P('fsdp'), may hold values from -9 to -1
- a_log: bfloat16 [48], P('fsdp'), may hold values from -3 to 1.5
- skip_d: bfloat16 [48], P('fsdp'), may hold values from 0.5 to 1.5
- inner_gain: bfloat16 [3072], P('fsdp'), may hold values from 0.5 to 1.5
- out_weight: bfloat16 [3072, 1536], P('fsdp'), may hold values from -0.109375 to 0.109375
Outputs:
- block_out: float32 [4, 2048, 1536], P('fsdp', 'seq')
- grad_hidden: float32 [4, 2048, 1536], P('fsdp', 'seq')
- grad_norm_gain: float32 [1536], P('fsdp')
- grad_in_weight: float32 [1536, 6448], P('fsdp')
- grad_conv_weight: float32 [3328, 4], P('fsdp')
- grad_conv_bias: float32 [3328], P('fsdp')
- grad_dt_bias: float32 [48], P('fsdp')
- grad_a_log: float32 [48], P('fsdp')
- grad_skip_d: float32 [48], P('fsdp')
- grad_inner_gain: float32 [3072], P('fsdp')
- grad_out_weight: float32 [3072, 1536], P('fsdp')
The draws below stay inside these ranges and needn't reach their ends.
All inputs are finite; a program needn't handle non-finite values.
Results may differ from the reference program's by a relative error of at most 0.0049.
The reference program's roundings to bfloat16 on the way count: a program that leaves them out, or rounds other values in their place, can miss the bound.
Values may be sent and summed in bfloat16 or wider, within the bound.
No kernel may reach another device: no remote copies, remote signals or barrier semaphores. Data moves between devices by JAX's collectives and lax.ppermute only.
A program may use at most 384 MiB of HBM per device.

```python
import jax
import jax.numpy as jnp
from jax import lax

D = 1536
KCONV = 4
SPAN = 256
DI = 3072
H = 48
CONVW = 3328
PROJ = 6448
LEN = 2048
SEQS = 4


def levels(key, extent, pieces, smallest, top_value):
    level = 1.0
    for position, shards_of in pieces:
        heights = jax.random.uniform(jax.random.fold_in(jax.random.fold_in(key, 6), position), (shards_of,), jnp.float32, smallest / len(pieces), top_value / len(pieces))
        level = level * jnp.repeat(jnp.exp(heights), extent[position] // shards_of).reshape((-1,) + (1,) * (len(extent) - 1 - position))
    return level


def noise(own_key, extent, scale, reach, shards=(), dtype=jnp.bfloat16):
    drawn = scale * jax.random.normal(own_key, extent, jnp.float32)
    if shards:
        drawn = drawn * levels(own_key, extent, shards, -0.22, 0.18)
    return jnp.clip(drawn, -reach, reach).astype(dtype)


def setup_inputs(seed: int = 0) -> dict:
    key_list = jax.random.split(jax.random.key(seed), 12)
    return {
        "hidden": noise(key_list[0], (SEQS, LEN, D), 1.0, 6.0, ((0, 4), (1, 8))),
        "cotangent": noise(key_list[1], (SEQS, LEN, D), 1.0, 6.0, ((0, 4), (1, 8))),
        "norm_gain": jnp.clip(1.0 + 0.1 * jax.random.normal(key_list[2], (D,), jnp.float32), 0.5, 1.5).astype(jnp.bfloat16),
        "in_weight": noise(key_list[3], (D, PROJ), D ** -0.5, 0.15625, ((0, 4),)),
        "conv_weight": noise(key_list[4], (CONVW, KCONV), KCONV ** -0.5, 3.0, ((0, 4),)),
        "conv_bias": noise(key_list[5], (CONVW,), 0.5, 3.0, ((0, 4),)),
        "dt_bias": jnp.clip(-9.0 + 8.0 * jax.random.uniform(key_list[6], (H,), jnp.float32) ** levels(key_list[6], (H,), ((0, 4),), -0.2, 0.2), -9.0, -1.0).astype(jnp.bfloat16),
        "a_log": jnp.clip(-3.0 + 4.5 * jax.random.uniform(key_list[7], (H,), jnp.float32) ** levels(key_list[7], (H,), ((0, 4),), -0.2, 0.2), -3.0, 1.5).astype(jnp.bfloat16),
        "skip_d": jnp.clip(0.5 + 1.0 * jax.random.uniform(key_list[8], (H,), jnp.float32) ** levels(key_list[8], (H,), ((0, 4),), -0.2, 0.2), 0.5, 1.5).astype(jnp.bfloat16),
        "inner_gain": jnp.clip(1.0 + 0.1 * jax.random.normal(key_list[9], (DI,), jnp.float32), 0.5, 1.5).astype(jnp.bfloat16),
        "out_weight": noise(key_list[10], (DI, D), DI ** -0.5, 0.109375, ((0, 4),)),
    }


def rms_norm(values, gain_vec):
    scale = lax.rsqrt(lax.optimization_barrier(jnp.mean(values * values, axis=-1, keepdims=True)) + 1e-05)
    return values * scale * gain_vec

def gated_norm(mixed, gate_in, gain_vec):
    gated = mixed * jax.nn.silu(gate_in)
    return rms_norm(gated, gain_vec)

def conv_silu(padded, weight, shift_bias):
    out_rows = padded.shape[0] - weight.shape[1] + 1
    running = shift_bias[None, :] + padded[0:out_rows] * weight[:, 0]
    for offset in range(1, weight.shape[1]):
        running = running + padded[offset:offset + out_rows] * weight[:, offset]
    return jax.nn.silu(running)

def ssd_scan(inputs_x, raw_step, bc_rows, log_rate, step_bias, skip_vec):
    seq_len, head_count = raw_step.shape
    head_width = inputs_x.shape[1] // head_count
    state_width = bc_rows.shape[1] // 2
    block_count = seq_len // SPAN
    step_size = jax.nn.softplus(raw_step + step_bias)
    decay_rate = -jnp.exp(log_rate)
    x_blocks = inputs_x.reshape(block_count, SPAN, head_count, head_width)
    step_blocks = step_size.reshape(block_count, SPAN, head_count)
    b_blocks = bc_rows[:, :state_width].reshape(block_count, SPAN, state_width)
    c_blocks = bc_rows[:, state_width:].reshape(block_count, SPAN, state_width)
    lower_mask = (jnp.arange(SPAN)[:, None] >= jnp.arange(SPAN)[None, :])[:, :, None]
    highest = lax.Precision.HIGHEST

    def advance(carry_state, block_in):
        x_block, step_block, b_block, c_block = block_in
        log_decay = jnp.cumsum(step_block * decay_rate, axis=0)
        log_gap = log_decay[:, None, :] - log_decay[None, :, :]
        decay_mat = jnp.where(lower_mask, jnp.exp(jnp.where(lower_mask, log_gap, 0.0)), 0.0)
        intersection = jnp.dot(c_block, b_block.T, precision=highest)
        mixing = intersection[:, :, None] * decay_mat * step_block[None, :, :]
        local_part = jnp.einsum('ijh,jhp->ihp', mixing, x_block, precision=highest)
        carried = jnp.einsum('in,hnp->ihp', c_block, carry_state, precision=highest) * jnp.exp(log_decay)[:, :, None]
        to_end = jnp.exp(log_decay[-1][None, :] - log_decay) * step_block
        fresh = jnp.einsum('jn,jh,jhp->hnp', b_block, to_end, x_block, precision=highest)
        next_state = carry_state * jnp.exp(log_decay[-1])[:, None, None] + fresh
        output = local_part + carried + skip_vec[None, :, None] * x_block
        return (next_state, output)
    start_state = jnp.zeros((head_count, state_width, head_width), jnp.float32)
    _, outputs = lax.scan(jax.checkpoint(advance), start_state, (x_blocks, step_blocks, b_blocks, c_blocks))
    return outputs.reshape(seq_len, head_count * head_width)

def across_rows(left, right):
    return lax.dot_general(left, right, (((0,), (0,)), ((), ())), preferred_element_type=jnp.float32)

def against_cols(left, right):
    return lax.dot_general(left, right, (((1,), (1,)), ((), ())), preferred_element_type=jnp.float32)

def rounded(values):
    return lax.optimization_barrier(values.astype(jnp.bfloat16)).astype(jnp.float32)

def sequence_pass(params, hidden_seq, cot_seq):
    gain_n, w_in, w_conv, b_conv, bias_dt, log_a, skip_vec, gain_i, w_out = params
    hidden_f = hidden_seq.astype(jnp.float32)
    normed, norm_pull = jax.vjp(rms_norm, hidden_f, gain_n)
    normed_b = normed.astype(jnp.bfloat16)
    projected = jnp.dot(normed_b, w_in, preferred_element_type=jnp.float32)
    proj_f = rounded(projected)
    gate_in = proj_f[:, :DI]
    conv_in = proj_f[:, DI:DI + CONVW]
    raw_step = proj_f[:, DI + CONVW:]
    padded = jnp.concatenate([jnp.zeros((KCONV - 1, CONVW), jnp.float32), conv_in], 0)
    conv_out, conv_pull = jax.vjp(conv_silu, padded, w_conv, b_conv)
    conv_f = rounded(conv_out)
    mixed, ssd_pull = jax.vjp(ssd_scan, conv_f[:, :DI], raw_step, conv_f[:, DI:], log_a, bias_dt, skip_vec)
    gated, gate_pull = jax.vjp(gated_norm, rounded(mixed), gate_in, gain_i)
    gated_b = gated.astype(jnp.bfloat16)
    block_out = hidden_f + jnp.dot(gated_b, w_out, preferred_element_type=jnp.float32)
    grad_w_out = across_rows(gated_b, cot_seq)
    d_gated = against_cols(cot_seq, w_out)
    d_mixed, d_gate, grad_gain_i = gate_pull(d_gated)
    d_x, d_step, d_bc, grad_log_a, grad_bias_dt, grad_skip = ssd_pull(rounded(d_mixed))
    d_conv = jnp.concatenate([rounded(d_x), d_bc], 1)
    d_padded, grad_w_conv, grad_b_conv = conv_pull(d_conv)
    d_proj = jnp.concatenate([d_gate, d_padded[KCONV - 1:], rounded(d_step)], 1).astype(jnp.bfloat16)
    grad_w_in = across_rows(normed_b, d_proj)
    d_normed = against_cols(d_proj, w_in)
    d_hidden, grad_gain_n = norm_pull(d_normed)
    grad_hidden = cot_seq.astype(jnp.float32) + d_hidden
    grads = (grad_gain_n, grad_w_in, grad_w_conv, grad_b_conv, grad_bias_dt, grad_log_a, grad_skip, grad_gain_i, grad_w_out)
    return (block_out, grad_hidden, grads)

def add_pair(first, second):
    return first + second

def make_zeros(param):
    return jnp.zeros(param.shape, jnp.float32)

def reference(hidden, cotangent, norm_gain, in_weight, conv_weight, conv_bias, dt_bias, a_log, skip_d, inner_gain, out_weight):
    params = (norm_gain.astype(jnp.float32), in_weight, conv_weight.astype(jnp.float32), conv_bias.astype(jnp.float32), dt_bias.astype(jnp.float32), a_log.astype(jnp.float32), skip_d.astype(jnp.float32), inner_gain.astype(jnp.float32), out_weight)

    def scan_step(carry, pair):
        block_out, grad_hidden, grads = sequence_pass(params, pair[0], pair[1])
        return (jax.tree.map(add_pair, carry, grads), (block_out, grad_hidden))
    start = jax.tree.map(make_zeros, params)
    sums, outputs = lax.scan(scan_step, start, (hidden, cotangent))
    return (outputs[0], outputs[1], sums[0], sums[1], sums[2], sums[3], sums[4], sums[5], sums[6], sums[7], sums[8])
```

```python
import functools

import jax
import jax.numpy as jnp
from jax import lax
from jax.experimental import pallas as pl
from jax.experimental.pallas import tpu as pltpu
from jax.sharding import PartitionSpec as P


EPS = 1e-05
LANES = 128
GROUP = 8
WIDE = True
BF16 = jnp.bfloat16
F32 = jnp.float32
HIGHEST = lax.Precision.HIGHEST


def dims(left, right, contract):
    return lax.dot_general(left, right, (contract, ((), ())), preferred_element_type=F32)


def across_rows(left, right):
    return dims(left, right, ((0,), (0,)))


def against_cols(left, right):
    return dims(left, right, ((1,), (1,)))


def plain_dot(left, right):
    return dims(left, right, ((1,), (0,)))


def halves(values):
    high = values.astype(BF16)
    return high, (values - high.astype(F32)).astype(BF16)


def rounded(values):
    return lax.reduce_precision(values, 8, 7)


def host_halves(values):
    high = rounded(values)
    return high.astype(BF16), (values - high).astype(BF16)


def per_head_lanes(columns, first, head_width, rows):
    per_tile = LANES // head_width
    lane = lax.broadcasted_iota(jnp.int32, (rows, LANES), 1)
    spread = jnp.broadcast_to(columns[:, first : first + 1], (rows, LANES))
    for extra in range(1, per_tile):
        column = columns[:, first + extra : first + extra + 1]
        spread = jnp.where(lane < extra * head_width, spread, column)
    return spread


def state_kernel(head_width, x_ref, bt_ref, te_ref, out_ref):
    rows = x_ref.shape[0]
    te_cols = te_ref[...].T
    per_tile = LANES // head_width
    for tile in range(x_ref.shape[1] // LANES):
        lanes = slice(tile * LANES, (tile + 1) * LANES)
        spread = per_head_lanes(te_cols, tile * per_tile, head_width, rows)
        high, low = halves(x_ref[:, lanes].astype(F32) * spread)
        out_ref[:, lanes] = plain_dot(bt_ref[...], high) + plain_dot(bt_ref[...], low)


def local_state(x_rows, b_cols, to_end, head_width):
    rows, width = x_rows.shape
    states = b_cols.shape[0]
    block = GROUP * head_width
    return pl.pallas_call(
        functools.partial(state_kernel, head_width),
        out_shape=jax.ShapeDtypeStruct((states, width), F32),
        grid=(width // block,),
        in_specs=[
            pl.BlockSpec((rows, block), lambda g: (0, g)),
            pl.BlockSpec((states, rows), lambda g: (0, 0)),
            pl.BlockSpec((GROUP, rows), lambda g: (g, 0)),
        ],
        out_specs=pl.BlockSpec((states, block), lambda g: (0, g)),
        name="local_state",
    )(x_rows, b_cols, to_end)


def tile_exponent(row_part, col_part, diagonal, lower):
    gap = row_part - col_part if lower else col_part - row_part
    if diagonal:
        first = lax.broadcasted_iota(jnp.int32, gap.shape, 0)
        second = lax.broadcasted_iota(jnp.int32, gap.shape, 1)
        keep = first >= second if not lower else second >= first
        gap = jnp.where(keep, gap, -1e30)
    return jnp.exp(gap)


def inner_kernel(head_width, x_ref, b_ref, c_ref, decay_ref, source_ref, out_ref, meet_ref):
    rows = x_ref.shape[0]
    tiles = rows // LANES

    @pl.when(pl.program_id(0) == 0)
    def _():
        meet_ref[...] = against_cols(c_ref[...], b_ref[...])

    decay_cols = decay_ref[...].T
    for late in range(tiles):
        out_rows = slice(late * LANES, (late + 1) * LANES)
        for head in range(GROUP):
            lanes = slice(head * head_width, (head + 1) * head_width)
            total = None
            for early in range(late + 1):
                in_rows = slice(early * LANES, (early + 1) * LANES)
                weight = tile_exponent(
                    source_ref[head : head + 1, in_rows],
                    decay_cols[out_rows, head : head + 1],
                    early == late,
                    False,
                )
                high, low = halves(meet_ref[out_rows, in_rows] * weight)
                x_now = x_ref[in_rows, lanes]
                part = plain_dot(high, x_now) + plain_dot(low, x_now)
                total = part if total is None else total + part
            out_ref[out_rows, lanes] = total


def inner_part(x_rows, b_rows, c_rows, decay, source, head_width):
    rows, width = x_rows.shape
    states = b_rows.shape[1]
    block = GROUP * head_width
    return pl.pallas_call(
        functools.partial(inner_kernel, head_width),
        out_shape=jax.ShapeDtypeStruct((rows, width), F32),
        grid=(width // block,),
        in_specs=[
            pl.BlockSpec((rows, block), lambda g: (0, g)),
            pl.BlockSpec((rows, states), lambda g: (0, 0)),
            pl.BlockSpec((rows, states), lambda g: (0, 0)),
            pl.BlockSpec((GROUP, rows), lambda g: (g, 0)),
            pl.BlockSpec((GROUP, rows), lambda g: (g, 0)),
        ],
        out_specs=pl.BlockSpec((rows, block), lambda g: (0, g)),
        scratch_shapes=[pltpu.VMEM((rows, rows), F32)],
        name="inner_part",
    )(x_rows, b_rows, c_rows, decay, source)


def middle_kernel(
    inner_ref,
    x_ref,
    gate_ref,
    dgated_ref,
    c_ref,
    state_ref,
    rest_ref,
    decay_ref,
    spread_ref,
    fold_ref,
    skip_ref,
    gain_ref,
    gated_ref,
    dmixed_ref,
    dgate_ref,
    dstate_ref,
    rowsum_ref,
    dgain_ref,
    dskip_ref,
):
    @pl.when(pl.program_id(0) == 0)
    def _():
        dstate_ref[...] = jnp.zeros_like(dstate_ref)
        dgain_ref[...] = jnp.zeros_like(dgain_ref)
        dskip_ref[...] = jnp.zeros_like(dskip_ref)

    decay = plain_dot(decay_ref[...], spread_ref[...])
    carried = plain_dot(c_ref[...], state_ref[...]) + plain_dot(c_ref[...], rest_ref[...])
    scanned = inner_ref[...] + carried * decay
    x_now = x_ref[...].astype(F32)
    mixed = (scanned + skip_ref[...] * x_now).astype(BF16).astype(F32)
    gate = gate_ref[...].astype(F32)
    sig = jax.nn.sigmoid(gate)
    act = gate * sig
    product = mixed * act
    scale = lax.rsqrt(jnp.mean(product * product, axis=-1, keepdims=True) + EPS)
    gain = gain_ref[...]
    unit = product * scale
    gated_ref[...] = (unit * gain).astype(BF16)
    d_gated = dgated_ref[...]
    dgain_ref[...] += jnp.sum(d_gated * unit, axis=0, keepdims=True)
    d_unit = d_gated * gain
    d_product = scale * (d_unit - unit * jnp.mean(d_unit * unit, axis=-1, keepdims=True))
    d_mixed_b = (d_product * act).astype(BF16)
    d_mixed = d_mixed_b.astype(F32)
    dmixed_ref[...] = d_mixed_b
    dgate_ref[...] = (d_product * mixed * (sig + act * (1.0 - sig))).astype(BF16)
    dskip_ref[...] += jnp.sum(d_mixed * x_now, axis=0, keepdims=True)
    high, low = halves(decay * d_mixed)
    dstate_ref[...] += across_rows(c_ref[...], high) + across_rows(c_ref[...], low)
    high, low = halves(d_mixed * scanned)
    rowsum_ref[...] = plain_dot(high, fold_ref[...]) + plain_dot(low, fold_ref[...])


def middle(inner, x_rows, gate, d_gated, c_rows, state, rest, decay, spread, fold, skip, gain, row_block):
    rows, width = x_rows.shape
    states, heads = c_rows.shape[1], fold.shape[1]
    blocked = lambda cols: pl.BlockSpec((row_block, cols), lambda i: (i, 0))
    whole = lambda array: pl.BlockSpec(array.shape, lambda i: (0, 0))
    kept = lambda *shape: pl.BlockSpec(shape, lambda i: (0, 0))
    return pl.pallas_call(
        middle_kernel,
        out_shape=(
            jax.ShapeDtypeStruct((rows, width), BF16),
            jax.ShapeDtypeStruct((rows, width), BF16),
            jax.ShapeDtypeStruct((rows, width), BF16),
            jax.ShapeDtypeStruct((states, width), F32),
            jax.ShapeDtypeStruct((rows, heads), F32),
            jax.ShapeDtypeStruct((1, width), F32),
            jax.ShapeDtypeStruct((1, width), F32),
        ),
        grid=(rows // row_block,),
        in_specs=[
            blocked(width),
            blocked(width),
            blocked(width),
            blocked(width),
            blocked(states),
            whole(state),
            whole(rest),
            blocked(decay.shape[1]),
            whole(spread),
            whole(fold),
            whole(skip),
            whole(gain),
        ],
        out_specs=(
            blocked(width),
            blocked(width),
            blocked(width),
            kept(states, width),
            blocked(heads),
            kept(1, width),
            kept(1, width),
        ),
        name="middle",
    )(inner, x_rows, gate, d_gated, c_rows, state, rest, decay, spread, fold, skip, gain)


def inner_grad_kernel(
    head_width,
    x_ref,
    dy_ref,
    b_ref,
    c_ref,
    decay_ref,
    source_ref,
    grown_ref,
    state_ref,
    dx_ref,
    dmeet_ref,
    dc_ref,
    meet_ref,
):
    rows = x_ref.shape[0]
    tiles = rows // LANES
    per_tile = LANES // head_width

    @pl.when(pl.program_id(0) == 0)
    def _():
        meet_ref[...] = against_cols(b_ref[...], c_ref[...])
        dmeet_ref[...] = jnp.zeros_like(dmeet_ref)
        dc_ref[...] = jnp.zeros_like(dc_ref)

    source_cols = source_ref[...].T
    grown_cols = grown_ref[...].T
    for early in range(tiles):
        in_rows = slice(early * LANES, (early + 1) * LANES)
        for late in range(early, tiles):
            out_rows = slice(late * LANES, (late + 1) * LANES)
            meet = meet_ref[in_rows, out_rows]
            total = dmeet_ref[in_rows, out_rows]
            for head in range(GROUP):
                lanes = slice(head * head_width, (head + 1) * head_width)
                weight = tile_exponent(
                    decay_ref[head : head + 1, out_rows],
                    source_cols[in_rows, head : head + 1],
                    early == late,
                    True,
                )
                dy = dy_ref[out_rows, lanes]
                high, low = halves(meet * weight)
                part = plain_dot(high, dy) + plain_dot(low, dy)
                if late == early:
                    dx_ref[in_rows, lanes] = part
                else:
                    dx_ref[in_rows, lanes] += part
                total = total + against_cols(x_ref[in_rows, lanes], dy) * weight
            dmeet_ref[in_rows, out_rows] = total
    for tile in range(x_ref.shape[1] // LANES):
        lanes = slice(tile * LANES, (tile + 1) * LANES)
        spread = per_head_lanes(grown_cols, tile * per_tile, head_width, rows)
        scaled = (dy_ref[:, lanes].astype(F32) * spread).astype(BF16)
        dc_ref[...] += against_cols(scaled, state_ref[:, lanes])


def inner_grad(x_rows, dy, b_rows, c_rows, decay, source, grown, state, head_width):
    rows, width = x_rows.shape
    states = b_rows.shape[1]
    block = GROUP * head_width
    group_rows = pl.BlockSpec((GROUP, rows), lambda g: (g, 0))
    return pl.pallas_call(
        functools.partial(inner_grad_kernel, head_width),
        out_shape=(
            jax.ShapeDtypeStruct((rows, width), F32),
            jax.ShapeDtypeStruct((rows, rows), F32),
            jax.ShapeDtypeStruct((rows, states), F32),
        ),
        grid=(width // block,),
        in_specs=[
            pl.BlockSpec((rows, block), lambda g: (0, g)),
            pl.BlockSpec((rows, block), lambda g: (0, g)),
            pl.BlockSpec((rows, states), lambda g: (0, 0)),
            pl.BlockSpec((rows, states), lambda g: (0, 0)),
            group_rows,
            group_rows,
            group_rows,
            pl.BlockSpec((states, block), lambda g: (0, g)),
        ],
        out_specs=(
            pl.BlockSpec((rows, block), lambda g: (0, g)),
            pl.BlockSpec((rows, rows), lambda g: (0, 0)),
            pl.BlockSpec((rows, states), lambda g: (0, 0)),
        ),
        scratch_shapes=[pltpu.VMEM((rows, rows), F32)],
        name="inner_grad",
    )(x_rows, dy, b_rows, c_rows, decay, source, grown, state)


def outer_grad_kernel(
    inner_ref,
    x_ref,
    dy_ref,
    b_ref,
    dstate_ref,
    toend_ref,
    spread_ref,
    fold_ref,
    skip_ref,
    dx_ref,
    colsum_ref,
    endsum_ref,
    db_ref,
):
    to_end = plain_dot(toend_ref[...], spread_ref[...])
    x_now = x_ref[...].astype(F32)
    through = to_end * plain_dot(b_ref[...], dstate_ref[...])
    d_scanned = inner_ref[...] + through
    dx_ref[...] = (d_scanned + skip_ref[...] * dy_ref[...].astype(F32)).astype(BF16)
    fold = fold_ref[...]
    high, low = halves(x_now * d_scanned)
    colsum_ref[...] = plain_dot(high, fold) + plain_dot(low, fold)
    high, low = halves(x_now * through)
    endsum_ref[...] = plain_dot(high, fold) + plain_dot(low, fold)
    db_ref[...] = against_cols((to_end * x_now).astype(BF16), dstate_ref[...])


def outer_grad(inner, x_rows, dy, b_rows, dstate, to_end, spread, fold, skip, row_block):
    rows, width = x_rows.shape
    states, heads = b_rows.shape[1], fold.shape[1]
    blocked = lambda cols: pl.BlockSpec((row_block, cols), lambda i: (i, 0))
    whole = lambda array: pl.BlockSpec(array.shape, lambda i: (0, 0))
    return pl.pallas_call(
        outer_grad_kernel,
        out_shape=(
            jax.ShapeDtypeStruct((rows, width), BF16),
            jax.ShapeDtypeStruct((rows, heads), F32),
            jax.ShapeDtypeStruct((rows, heads), F32),
            jax.ShapeDtypeStruct((rows, states), F32),
        ),
        grid=(rows // row_block,),
        in_specs=[
            blocked(width),
            blocked(width),
            blocked(width),
            blocked(states),
            whole(dstate),
            blocked(to_end.shape[1]),
            whole(spread),
            whole(fold),
            whole(skip),
        ],
        out_specs=(blocked(width), blocked(heads), blocked(heads), blocked(states)),
        name="outer_grad",
    )(inner, x_rows, dy, b_rows, dstate, to_end, spread, fold, skip)


def passed_along(value, axis, steps):
    count = lax.axis_size(axis)
    first, last = (max(0, -steps), min(count, count - steps))
    return lax.ppermute(value, axis, [(source, source + steps) for source in range(first, last)])


def three_parts(values):
    first = rounded(values)
    second = rounded(values - first)
    return first.astype(BF16), second.astype(BF16), (values - first - second).astype(BF16)


def carried_states(local, log_total, axis, backward, beside=None):
    count = lax.axis_size(axis)
    states, width = local.shape
    part = width // count
    wire = BF16 if backward or not WIDE else F32
    logs = three_parts(log_total) if wire == BF16 else (log_total,)
    packed = jnp.concatenate([local.astype(wire), *(p[None] for p in logs)], 0)
    split = packed.reshape(packed.shape[0], count, part).transpose(1, 0, 2)
    held = lax.all_to_all(split, axis, split_axis=0, concat_axis=0, tiled=True)
    if beside is not None:
        held = after(held, beside)
    own = held[:, :states].astype(F32)
    logs = jnp.sum(held[:, states:].astype(F32), axis=1)
    decay = jnp.exp(logs)
    order = range(count - 1, -1, -1) if backward else range(count)
    running = jnp.zeros((states, part), F32)
    entering = [None] * count
    for device in order:
        entering[device] = running.astype(wire)
        running = running * decay[device][None, :] + own[device]
    home = lax.all_to_all(jnp.stack(entering), axis, split_axis=0, concat_axis=0, tiled=True)
    return home


def joined(home):
    count, states, part = home.shape
    return home.transpose(1, 0, 2).reshape(states, count * part)


def swapped(value, axis, mask):
    count = lax.axis_size(axis)
    return lax.ppermute(value, axis, [(source, source ^ mask) for source in range(count)])


def flip_order(count):
    order = [0]
    mask = count // 2
    while mask:
        order += [flip ^ mask for flip in order]
        mask //= 2
    return order


def gathered(value, axis):
    first = []
    mask = lax.axis_size(axis) // 2
    while mask:
        first.append(swapped(value, axis, mask))
        mask //= 2
    return value, first


def passed_on(started, axis, held_for=None):
    value, first = started
    if held_for is not None:
        first = after(first, held_for)
    blocks = [value]
    mask = lax.axis_size(axis) // 2
    for arrived in first:
        blocks += [arrived] + [swapped(block, axis, mask) for block in blocks[1:]]
        mask //= 2
    return blocks


def after(value, earlier):
    return lax.optimization_barrier((value, earlier))[0]


def weight_parts(shard, side):
    place = lax.axis_index(side) % 2
    rows = shard.shape[0]
    third = rows // 3 // 16 * 16
    alone = rows - 2 * third
    return (alone + place * third, 0, alone + (1 - place) * third), (third, alone, third)


def weight_sent(shard, axis, side):
    offsets, sizes = weight_parts(shard, side)
    shared, own = (
        lax.dynamic_slice_in_dim(shard, o, n, 0) for o, n in zip(offsets[:2], sizes[:2])
    )
    mask = lax.axis_size(axis) // 2
    if mask == 1:
        return (swapped(shard, axis, 1),)
    arrived = swapped(shared, axis, mask)
    return swapped(shard, axis, 1), arrived, swapped(own, axis, mask)


def weight_gathered(shard, sent, axis, side):
    count, rank = lax.axis_size(axis), lax.axis_index(axis)
    rows = shard.shape[0]
    offsets, sizes = weight_parts(shard, side)
    held = {0: tuple(lax.dynamic_slice_in_dim(shard, o, n, 0) for o, n in zip(offsets, sizes))}
    whole = jnp.zeros((count * rows, shard.shape[1]), shard.dtype)
    mask = count // 2
    while mask > 1:
        for flip, (shared, own, _) in tuple(held.items()):
            if flip or mask < count // 2:
                arrived, direct = swapped(shared, axis, mask), swapped(own, axis, mask)
            else:
                arrived, direct = sent[1:]
            held[flip ^ mask] = (arrived, direct, swapped(arrived, side, 1))
        mask //= 2
    for flip, block in ((0, shard), (1, sent[0])):
        whole = lax.dynamic_update_slice_in_dim(whole, block, (rank ^ flip) * rows, 0)
    for flip, blocks in held.items():
        if flip:
            for block, offset in zip(blocks, offsets):
                start = (rank ^ flip) * rows + offset
                whole = lax.dynamic_update_slice_in_dim(whole, block, start, 0)
                start = (rank ^ flip ^ 1) * rows + offset
                whole = lax.dynamic_update_slice_in_dim(whole, swapped(block, axis, 1), start, 0)
    return whole


def exchanged(value, axis):
    count, rank = lax.axis_size(axis), lax.axis_index(axis)
    part = value.shape[1] // count
    blocks = []
    for flip in flip_order(count):
        piece = lax.dynamic_slice_in_dim(value, (rank ^ flip) * part, part, 1)
        blocks.append(swapped(piece, axis, flip) if flip else piece)
    return blocks


def product_kernel(place_ref, *refs):
    count = (len(refs) - 3) // 2
    left_refs, right_refs = refs[:count], refs[count : 2 * count]
    near_ref, away_ref, turned_ref = refs[2 * count :]
    tokens = left_refs[0].shape[0]

    @pl.when(pl.program_id(0) == 0)
    def _():
        for index, left_ref in enumerate(left_refs):
            turned_ref[:, index * tokens : (index + 1) * tokens] = left_ref[...].T

    half = near_ref.shape[0]
    for upper in range(2):
        rows = slice(upper * half, (upper + 1) * half)
        total = None
        for index, right_ref in enumerate(right_refs):
            part = plain_dot(
                turned_ref[rows, index * tokens : (index + 1) * tokens], right_ref[...]
            )
            total = part if total is None else total + part

        @pl.when(place_ref[0] == upper)
        def _():
            near_ref[...] = total

        @pl.when(place_ref[0] != upper)
        def _():
            away_ref[...] = total.astype(BF16)


def weight_product(lefts, rights, axis):
    place = (lax.axis_index(axis) % 2).astype(jnp.int32).reshape(1)
    tokens, rows = lefts[0].shape
    width = rights[0].shape[1]
    block = 512
    return pl.pallas_call(
        product_kernel,
        out_shape=(
            jax.ShapeDtypeStruct((rows // 2, width), F32),
            jax.ShapeDtypeStruct((rows // 2, width), BF16),
        ),
        grid_spec=pltpu.PrefetchScalarGridSpec(
            num_scalar_prefetch=1,
            grid=(pl.cdiv(width, block),),
            in_specs=[pl.BlockSpec((tokens, rows), lambda i, place: (0, 0)) for _ in lefts]
            + [pl.BlockSpec((tokens, block), lambda i, place: (0, i)) for _ in rights],
            out_specs=tuple(
                pl.BlockSpec((rows // 2, block), lambda i, place: (0, i)) for _ in range(2)
            ),
            scratch_shapes=[pltpu.VMEM((rows, tokens * len(lefts)), BF16)],
        ),
        name="weight_product",
    )(place, *lefts, *rights)


def seq_owned(near, arrived, axis):
    count, rank = lax.axis_size(axis), lax.axis_index(axis)
    line = rank // 2
    block = near.shape[0] // (count // 2)
    pair = near + arrived.astype(F32)
    total = lax.dynamic_slice_in_dim(pair, line * block, block, 0)
    for flip in range(1, count // 2):
        piece = lax.dynamic_slice_in_dim(pair, (line ^ flip) * block, block, 0).astype(BF16)
        total = total + swapped(piece, axis, 2 * flip).astype(F32)
    return total.astype(BF16)


def seq_spread(owned, axis):
    count = lax.axis_size(axis)
    blocks = [owned] + [swapped(owned, axis, 2 * flip) for flip in range(1, count // 2)]
    mine = jnp.stack(blocks)
    return mine, swapped(mine, axis, 1)


def place_kernel(ranks_ref, *refs):
    out_ref = refs[-1]
    count = pl.num_programs(0)
    mine = pl.program_id(0) // (count // 2) == ranks_ref[0]
    cursor = 0
    for pair in range(len(refs) // 2):
        near_ref, far_ref = refs[2 * pair], refs[2 * pair + 1]
        width = min(near_ref.shape[2], out_ref.shape[-1] - cursor)

        @pl.when(mine)
        def _():
            out_ref[..., cursor : cursor + width] = near_ref[:, :, :width].astype(F32).reshape(
                (*out_ref.shape[:-1], width)
            )

        @pl.when(jnp.logical_not(mine))
        def _():
            out_ref[..., cursor : cursor + width] = far_ref[:, :, :width].astype(F32).reshape(
                (*out_ref.shape[:-1], width)
            )

        cursor += width


def placed(spreads, axis, width):
    count, rank = lax.axis_size(axis), lax.axis_index(axis)
    ranks = jnp.stack([rank % 2, rank // 2]).astype(jnp.int32)
    flat = [array for pair in spreads for array in pair]
    rows = flat[0].shape[1]
    pick = lambda i, ranks: ((i % (count // 2)) ^ ranks[1], 0, 0)
    if rows % 8:
        shape, out_spec = (count, rows, width), pl.BlockSpec((1, rows, width), lambda i, r: (i, 0, 0))
    else:
        shape, out_spec = (count * rows, width), pl.BlockSpec((rows, width), lambda i, r: (i, 0))
    out = pl.pallas_call(
        place_kernel,
        out_shape=jax.ShapeDtypeStruct(shape, F32),
        grid_spec=pltpu.PrefetchScalarGridSpec(
            num_scalar_prefetch=1,
            grid=(count,),
            in_specs=[pl.BlockSpec((1, rows, a.shape[2]), pick) for a in flat],
            out_specs=out_spec,
        ),
        name="placed",
    )(ranks, *flat)
    return out.reshape(count * rows, width)


def turned_kernel(ranks_ref, near_a_ref, far_a_ref, near_b_ref, far_b_ref, out_ref, held_ref):
    line, rows = near_a_ref.shape[0], near_a_ref.shape[1]

    def fill(near_ref, far_ref):
        for index in range(2 * line):
            source = (index % line) ^ ranks_ref[1]
            mine = ranks_ref[0] == index // line
            block = jnp.where(mine, near_ref[source].astype(F32), far_ref[source].astype(F32))
            held_ref[index * rows : (index + 1) * rows, :] = block

    first = pl.program_id(0) < ranks_ref[2]

    @pl.when(first)
    def _():
        fill(near_a_ref, far_a_ref)

    @pl.when(jnp.logical_not(first))
    def _():
        fill(near_b_ref, far_b_ref)

    out_ref[...] = held_ref[...].T


def placed_turned(first, second, axis, width):
    count, rank = lax.axis_size(axis), lax.axis_index(axis)
    rows, columns = first[0].shape[1:]
    block = next(b for b in (512, 256, 128) if columns % b == 0)
    ahead = columns // block
    ranks = jnp.stack([rank % 2, rank // 2, ahead]).astype(jnp.int32)
    shape = (count // 2, rows, block)
    first_spec = pl.BlockSpec(shape, lambda j, r: (0, 0, jnp.minimum(j, ahead - 1)))
    second_spec = pl.BlockSpec(shape, lambda j, r: (0, 0, jnp.maximum(j - ahead, 0)))
    return pl.pallas_call(
        turned_kernel,
        out_shape=jax.ShapeDtypeStruct((width, count * rows), F32),
        grid_spec=pltpu.PrefetchScalarGridSpec(
            num_scalar_prefetch=1,
            grid=(pl.cdiv(width, block),),
            in_specs=[first_spec, first_spec, second_spec, second_spec],
            out_specs=pl.BlockSpec((block, count * rows), lambda j, r: (j, 0)),
            scratch_shapes=[pltpu.VMEM((count * rows, block), F32)],
        ),
        name="placed_turned",
    )(ranks, *first, *second).T


def small_total(packed, split_axis, axis):
    count, rank = lax.axis_size(split_axis), lax.axis_index(split_axis)
    total = None
    for flip in flip_order(count):
        row = lax.dynamic_slice_in_dim(packed, rank ^ flip, 1, 0)
        row = swapped(row, split_axis, flip) if flip else row
        total = row if total is None else total + row
    mask = lax.axis_size(axis) // 2
    while mask:
        total = total + swapped(total, axis, mask)
        mask //= 2
    return total[0]


def body(
    hidden,
    cotangent,
    norm_gain,
    in_weight,
    conv_weight,
    conv_bias,
    dt_bias,
    a_log,
    skip_d,
    inner_gain,
    out_weight,
):
    owner_count = lax.axis_size("fsdp")
    taps = conv_weight.shape[1]
    model = hidden.shape[2]
    inner_width = inner_gain.shape[0] * owner_count
    heads = a_log.shape[0] * owner_count
    conv_width = conv_bias.shape[0] * owner_count
    states = (conv_width - inner_width) // 2
    head_width = inner_width // heads
    tokens = hidden.shape[1]
    row_block = 64

    small = jnp.concatenate(
        [
            norm_gain,
            inner_gain,
            conv_bias,
            conv_weight.T.reshape(-1),
            dt_bias,
            a_log,
            skip_d,
        ]
    )
    small = jnp.pad(small, (0, -small.shape[0] % LANES))
    small_held = jnp.stack(
        [swapped(small, "fsdp", flip) if flip else small for flip in range(owner_count)]
    )
    owner_rank = lax.axis_index("fsdp")
    small_all = jnp.concatenate(
        [
            lax.dynamic_slice_in_dim(small_held, owner_rank ^ owner, 1, 0)
            for owner in range(owner_count)
        ],
        0,
    )
    conv_shard, gate_shard = in_weight[:, inner_width:], in_weight[:, :inner_width]
    conv_sent = weight_sent(conv_shard, "fsdp", "seq")
    gate_sent = weight_sent(gate_shard, "fsdp", "seq")
    out_sent = weight_sent(out_weight, "fsdp", "seq")
    w_conv_in = weight_gathered(conv_shard, conv_sent, "fsdp", "seq")

    cursor = 0
    pieces = []
    for piece in (norm_gain, inner_gain, conv_bias, conv_weight, dt_bias, a_log, skip_d):
        pieces.append(small_all[:, cursor : cursor + piece.size].astype(F32))
        cursor += piece.size
    gain_n, gain_i, b_conv = (p.reshape(-1) for p in pieces[:3])
    w_taps = pieces[3].reshape(owner_count, taps, -1).transpose(1, 0, 2).reshape(taps, conv_width)
    bias_dt, log_a, skip_vec = (p.reshape(-1) for p in pieces[4:])

    hidden_f = hidden[0].astype(F32)
    cot_rows = cotangent[0]
    n_scale = lax.rsqrt(jnp.mean(hidden_f * hidden_f, axis=-1, keepdims=True) + EPS)
    n_unit = hidden_f * n_scale
    normed_b = (n_unit * gain_n).astype(BF16)

    stepped = plain_dot(normed_b, w_conv_in).astype(BF16)
    conv_in = stepped[:, :conv_width]
    raw_t = stepped[:, conv_width:].T.astype(F32)
    rim_rows = passed_along(conv_in[tokens - taps + 1 :], "seq", 1)
    gate_sent = after(gate_sent, rim_rows)
    w_gate = weight_gathered(gate_shard, gate_sent, "fsdp", "seq")
    padded = jnp.concatenate([rim_rows, conv_in], 0).astype(F32)
    pre_act = b_conv[None, :]
    for tap in range(taps):
        pre_act = pre_act + padded[tap : tap + tokens] * w_taps[tap]
    conv_act = jax.nn.silu(pre_act).astype(BF16)
    x_rows = conv_act[:, :inner_width]
    b_rows = conv_act[:, inner_width : inner_width + states]
    c_rows = conv_act[:, inner_width + states :]

    rate = -jnp.exp(log_a)[:, None]
    pre_step = raw_t + bias_dt[:, None]
    step = jax.nn.softplus(pre_step)
    ahead = jnp.triu(jnp.ones((tokens, tokens), F32))
    decay_log = jnp.dot(step * rate, ahead, precision=HIGHEST)
    source_log = decay_log - jnp.log(step)
    total_log = decay_log[:, -1]
    to_end = jnp.exp(total_log[:, None] - decay_log) * step
    grown = jnp.exp(decay_log)
    lane_head = jnp.arange(inner_width) // head_width
    one_hot = (jnp.arange(heads)[:, None] == lane_head[None, :]).astype(BF16)
    spread = jnp.concatenate([one_hot, one_hot], 0)
    fold = one_hot.T
    skip_lanes = jnp.repeat(skip_vec, head_width)[None, :]
    total_lanes = jnp.repeat(total_log, head_width)

    own_state = local_state(x_rows, b_rows.T, to_end, head_width)
    state_full = joined(carried_states(own_state, total_lanes, "seq", False))
    state_in = host_halves(state_full)
    inner = inner_part(after(x_rows, own_state), b_rows, c_rows, decay_log, source_log, head_width)
    out_sent = after(out_sent, inner)
    w_out = weight_gathered(out_weight, out_sent, "fsdp", "seq")
    sent = out_sent[-1]
    gate_in = plain_dot(normed_b, w_gate).astype(BF16)
    d_gated = against_cols(cot_rows, w_out)

    gated_b, d_mixed, d_gate, own_dstate, rowsum, grad_gain_i, skip_sums = middle(
        inner,
        x_rows,
        gate_in,
        d_gated,
        c_rows,
        *state_in,
        jnp.concatenate(host_halves(grown.T), 1),
        spread,
        fold,
        skip_lanes,
        gain_i[None, :],
        row_block,
    )
    normed_all = exchanged(after(normed_b, sent), "fsdp")
    cot_all = gathered(after(cot_rows, sent), "fsdp")
    gated_all = exchanged(gated_b, "fsdp")
    d_gate_all = gathered(d_gate, "fsdp")
    inner_dx, d_meet, dc_carried = inner_grad(
        x_rows, d_mixed, b_rows, c_rows, decay_log, source_log, grown, state_in[0], head_width
    )
    home = carried_states(own_dstate, total_lanes, "seq", True, inner_dx)
    cot_all = passed_on(cot_all, "fsdp")
    out_near, out_away = weight_product(gated_all, cot_all, "seq")
    out_arrived = swapped(out_away, "seq", 1)
    dstate = joined(after(home, out_near))
    d_x, colsum, endsum, db_carried = outer_grad(
        inner_dx,
        x_rows,
        d_mixed,
        b_rows,
        dstate,
        jnp.concatenate(host_halves(to_end.T), 1),
        spread,
        fold,
        skip_lanes,
        row_block,
    )
    d_gate_all = passed_on(d_gate_all, "fsdp", d_x)
    gate_near, gate_away = weight_product(normed_all, d_gate_all, "seq")
    gate_arrived = swapped(gate_away, "seq", 1)
    d_x = after(d_x, gate_near)
    d_meet_b = d_meet.astype(BF16)
    d_b = db_carried + plain_dot(d_meet_b, c_rows)
    d_c = dc_carried + across_rows(d_meet_b, b_rows)
    ends = jnp.sum(state_full * dstate.astype(F32), axis=0)
    ends = jnp.sum(ends.reshape(heads, head_width), axis=1) * jnp.exp(total_log)
    colsum_t = colsum.T
    d_log = rowsum.T - colsum_t
    d_last = jnp.sum(endsum, axis=0) + ends
    behind = jnp.tril(jnp.ones((tokens, tokens), F32))
    d_rate_step = jnp.dot(d_log, behind, precision=HIGHEST) + d_last[:, None]
    sig_step = jax.nn.sigmoid(pre_step)
    ratio = jnp.where(step > 0, sig_step / jnp.where(step > 0, step, 1.0), 0.0)
    d_raw = colsum_t * ratio + d_rate_step * rate * sig_step
    grad_log = jnp.sum(d_rate_step * step, axis=1) * rate[:, 0]
    grad_bias = jnp.sum(d_raw, axis=1)
    grad_skip = jnp.sum(skip_sums.reshape(heads, head_width), axis=1)

    d_conv = jnp.concatenate([d_x.astype(F32), d_b, d_c], 1)
    act_sig = jax.nn.sigmoid(pre_act)
    d_pre = d_conv * (act_sig * (1.0 + pre_act * (1.0 - act_sig)))
    after_rows = passed_along(d_pre[: taps - 1], "seq", -1)
    d_tail = jnp.concatenate([d_pre, after_rows], 0)
    d_conv_in = 0.0
    for tap in range(taps):
        shift = taps - 1 - tap
        d_conv_in = d_conv_in + d_tail[shift : shift + tokens] * w_taps[tap]
    spare = jnp.zeros((tokens, -(conv_width + heads) % LANES), BF16)
    d_step_proj = jnp.concatenate([d_conv_in.astype(BF16), d_raw.T.astype(BF16), spare], 1)
    d_step_all = passed_on(gathered(d_step_proj, "fsdp"), "fsdp")
    out_arrived = after(out_arrived, gate_near)
    out_spread = seq_spread(seq_owned(out_near, out_arrived, "seq"), "seq")
    gate_arrived = after(gate_arrived, d_step_proj)
    gate_spread = seq_spread(seq_owned(gate_near, gate_arrived, "seq"), "seq")
    step_near, step_away = weight_product(normed_all, d_step_all, "seq")
    step_arrived = swapped(step_away, "seq", 1)
    step_arrived = after(step_arrived, (gate_spread[0], out_spread[0]))
    step_spread = seq_spread(seq_owned(step_near, step_arrived, "seq"), "seq")
    d_pre = after(d_pre, d_step_proj)
    grad_w_conv = jnp.stack(
        [jnp.sum(d_pre * padded[tap : tap + tokens], axis=0) for tap in range(taps)]
    )
    grad_b_conv = jnp.sum(d_pre, axis=0)
    block_out = hidden_f + plain_dot(after(gated_b, d_step_proj), w_out)
    d_normed = against_cols(after(d_gate, d_step_proj), w_gate)
    d_normed = d_normed + against_cols(d_step_proj[:, : conv_width + heads], w_conv_in)
    d_unit = d_normed * gain_n
    d_hidden = n_scale * (d_unit - n_unit * jnp.mean(d_unit * n_unit, axis=-1, keepdims=True))
    grad_hidden = cot_rows.astype(F32) + d_hidden
    grad_gain_n = jnp.sum(d_normed * n_unit, axis=0)

    parts = (
        grad_gain_n,
        grad_gain_i[0],
        grad_b_conv,
        grad_bias,
        grad_log,
        grad_skip,
    )
    by_owner = [p.reshape(owner_count, -1) for p in parts]
    tap_part = grad_w_conv.reshape(taps, owner_count, -1).transpose(1, 0, 2)
    by_owner.append(tap_part.reshape(owner_count, -1))
    mine = small_total(jnp.concatenate(by_owner, 1), "fsdp", "seq")
    outs = []
    cursor = 0
    for part in by_owner:
        outs.append(mine[cursor : cursor + part.shape[1]])
        cursor += part.shape[1]
    return (
        block_out[None],
        grad_hidden[None],
        outs[0],
        placed_turned(gate_spread, step_spread, "seq", in_weight.shape[1]),
        outs[6].reshape(taps, -1).T,
        outs[2],
        outs[3],
        outs[4],
        outs[5],
        outs[1],
        placed((out_spread,), "seq", model),
    )


def solution(mesh):
    rows = P("fsdp", "seq", None)
    vector, matrix = P("fsdp"), P("fsdp", None)
    params = (vector, matrix, matrix, vector, vector, vector, vector, vector, matrix)
    return jax.shard_map(
        body,
        mesh=mesh,
        in_specs=(rows, rows, *params),
        out_specs=(rows, rows, *params),
        check_vma=False,
    )
```

```python
import functools

import jax
import jax.numpy as jnp
from jax import lax
from jax.experimental import pallas as pl
from jax.experimental.pallas import tpu as pltpu
from jax.sharding import PartitionSpec as P


EPS = 1e-05
LANES = 128
GROUP = 8
WIDE = True
BF16 = jnp.bfloat16
F32 = jnp.float32
HIGHEST = lax.Precision.HIGHEST


def dims(left, right, contract):
    return lax.dot_general(left, right, (contract, ((), ())), preferred_element_type=F32)


def across_rows(left, right):
    return dims(left, right, ((0,), (0,)))


def against_cols(left, right):
    return dims(left, right, ((1,), (1,)))


def plain_dot(left, right):
    return dims(left, right, ((1,), (0,)))


def halves(values):
    high = values.astype(BF16)
    return high, (values - high.astype(F32)).astype(BF16)


def rounded(values):
    return lax.reduce_precision(values, 8, 7)


def host_halves(values):
    high = rounded(values)
    return high.astype(BF16), (values - high).astype(BF16)


def per_head_lanes(columns, first, head_width, rows):
    per_tile = LANES // head_width
    lane = lax.broadcasted_iota(jnp.int32, (rows, LANES), 1)
    spread = jnp.broadcast_to(columns[:, first : first + 1], (rows, LANES))
    for extra in range(1, per_tile):
        column = columns[:, first + extra : first + extra + 1]
        spread = jnp.where(lane < extra * head_width, spread, column)
    return spread


def state_kernel(head_width, x_ref, bt_ref, te_ref, out_ref):
    rows = x_ref.shape[0]
    te_cols = te_ref[...].T
    per_tile = LANES // head_width
    for tile in range(x_ref.shape[1] // LANES):
        lanes = slice(tile * LANES, (tile + 1) * LANES)
        spread = per_head_lanes(te_cols, tile * per_tile, head_width, rows)
        high, low = halves(x_ref[:, lanes].astype(F32) * spread)
        out_ref[:, lanes] = plain_dot(bt_ref[...], high) + plain_dot(bt_ref[...], low)


def local_state(x_rows, b_cols, to_end, head_width):
    rows, width = x_rows.shape
    states = b_cols.shape[0]
    block = GROUP * head_width
    return pl.pallas_call(
        functools.partial(state_kernel, head_width),
        out_shape=jax.ShapeDtypeStruct((states, width), F32),
        grid=(width // block,),
        in_specs=[
            pl.BlockSpec((rows, block), lambda g: (0, g)),
            pl.BlockSpec((states, rows), lambda g: (0, 0)),
            pl.BlockSpec((GROUP, rows), lambda g: (g, 0)),
        ],
        out_specs=pl.BlockSpec((states, block), lambda g: (0, g)),
        name="local_state",
    )(x_rows, b_cols, to_end)


def tile_exponent(row_part, col_part, diagonal, lower):
    gap = row_part - col_part if lower else col_part - row_part
    if diagonal:
        first = lax.broadcasted_iota(jnp.int32, gap.shape, 0)
        second = lax.broadcasted_iota(jnp.int32, gap.shape, 1)
        keep = first >= second if not lower else second >= first
        gap = jnp.where(keep, gap, -1e30)
    return jnp.exp(gap)


def inner_kernel(head_width, x_ref, b_ref, c_ref, decay_ref, source_ref, out_ref, meet_ref):
    rows = x_ref.shape[0]
    tiles = rows // LANES

    @pl.when(pl.program_id(0) == 0)
    def _():
        meet_ref[...] = against_cols(c_ref[...], b_ref[...])

    decay_cols = decay_ref[...].T
    for late in range(tiles):
        out_rows = slice(late * LANES, (late + 1) * LANES)
        for head in range(GROUP):
            lanes = slice(head * head_width, (head + 1) * head_width)
            total = None
            for early in range(late + 1):
                in_rows = slice(early * LANES, (early + 1) * LANES)
                weight = tile_exponent(
                    source_ref[head : head + 1, in_rows],
                    decay_cols[out_rows, head : head + 1],
                    early == late,
                    False,
                )
                high, low = halves(meet_ref[out_rows, in_rows] * weight)
                x_now = x_ref[in_rows, lanes]
                part = plain_dot(high, x_now) + plain_dot(low, x_now)
                total = part if total is None else total + part
            out_ref[out_rows, lanes] = total


def inner_part(x_rows, b_rows, c_rows, decay, source, head_width):
    rows, width = x_rows.shape
    states = b_rows.shape[1]
    block = GROUP * head_width
    return pl.pallas_call(
        functools.partial(inner_kernel, head_width),
        out_shape=jax.ShapeDtypeStruct((rows, width), F32),
        grid=(width // block,),
        in_specs=[
            pl.BlockSpec((rows, block), lambda g: (0, g)),
            pl.BlockSpec((rows, states), lambda g: (0, 0)),
            pl.BlockSpec((rows, states), lambda g: (0, 0)),
            pl.BlockSpec((GROUP, rows), lambda g: (g, 0)),
            pl.BlockSpec((GROUP, rows), lambda g: (g, 0)),
        ],
        out_specs=pl.BlockSpec((rows, block), lambda g: (0, g)),
        scratch_shapes=[pltpu.VMEM((rows, rows), F32)],
        name="inner_part",
    )(x_rows, b_rows, c_rows, decay, source)


def middle_kernel(
    inner_ref,
    x_ref,
    gate_ref,
    dgated_ref,
    c_ref,
    state_ref,
    rest_ref,
    decay_ref,
    spread_ref,
    fold_ref,
    skip_ref,
    gain_ref,
    gated_ref,
    dmixed_ref,
    dgate_ref,
    dstate_ref,
    rowsum_ref,
    dgain_ref,
    dskip_ref,
):
    @pl.when(pl.program_id(0) == 0)
    def _():
        dstate_ref[...] = jnp.zeros_like(dstate_ref)
        dgain_ref[...] = jnp.zeros_like(dgain_ref)
        dskip_ref[...] = jnp.zeros_like(dskip_ref)

    decay = plain_dot(decay_ref[...], spread_ref[...])
    carried = plain_dot(c_ref[...], state_ref[...]) + plain_dot(c_ref[...], rest_ref[...])
    scanned = inner_ref[...] + carried * decay
    x_now = x_ref[...].astype(F32)
    mixed = (scanned + skip_ref[...] * x_now).astype(BF16).astype(F32)
    gate = gate_ref[...].astype(F32)
    sig = jax.nn.sigmoid(gate)
    act = gate * sig
    product = mixed * act
    scale = lax.rsqrt(jnp.mean(product * product, axis=-1, keepdims=True) + EPS)
    gain = gain_ref[...]
    unit = product * scale
    gated_ref[...] = (unit * gain).astype(BF16)
    d_gated = dgated_ref[...]
    dgain_ref[...] += jnp.sum(d_gated * unit, axis=0, keepdims=True)
    d_unit = d_gated * gain
    d_product = scale * (d_unit - unit * jnp.mean(d_unit * unit, axis=-1, keepdims=True))
    d_mixed_b = (d_product * act).astype(BF16)
    d_mixed = d_mixed_b.astype(F32)
    dmixed_ref[...] = d_mixed_b
    dgate_ref[...] = (d_product * mixed * (sig + act * (1.0 - sig))).astype(BF16)
    dskip_ref[...] += jnp.sum(d_mixed * x_now, axis=0, keepdims=True)
    high, low = halves(decay * d_mixed)
    dstate_ref[...] += across_rows(c_ref[...], high) + across_rows(c_ref[...], low)
    high, low = halves(d_mixed * scanned)
    rowsum_ref[...] = plain_dot(high, fold_ref[...]) + plain_dot(low, fold_ref[...])


def middle(inner, x_rows, gate, d_gated, c_rows, state, rest, decay, spread, fold, skip, gain, row_block):
    rows, width = x_rows.shape
    states, heads = c_rows.shape[1], fold.shape[1]
    blocked = lambda cols: pl.BlockSpec((row_block, cols), lambda i: (i, 0))
    whole = lambda array: pl.BlockSpec(array.shape, lambda i: (0, 0))
    kept = lambda *shape: pl.BlockSpec(shape, lambda i: (0, 0))
    return pl.pallas_call(
        middle_kernel,
        out_shape=(
            jax.ShapeDtypeStruct((rows, width), BF16),
            jax.ShapeDtypeStruct((rows, width), BF16),
            jax.ShapeDtypeStruct((rows, width), BF16),
            jax.ShapeDtypeStruct((states, width), F32),
            jax.ShapeDtypeStruct((rows, heads), F32),
            jax.ShapeDtypeStruct((1, width), F32),
            jax.ShapeDtypeStruct((1, width), F32),
        ),
        grid=(rows // row_block,),
        in_specs=[
            blocked(width),
            blocked(width),
            blocked(width),
            blocked(width),
            blocked(states),
            whole(state),
            whole(rest),
            blocked(decay.shape[1]),
            whole(spread),
            whole(fold),
            whole(skip),
            whole(gain),
        ],
        out_specs=(
            blocked(width),
            blocked(width),
            blocked(width),
            kept(states, width),
            blocked(heads),
            kept(1, width),
            kept(1, width),
        ),
        name="middle",
    )(inner, x_rows, gate, d_gated, c_rows, state, rest, decay, spread, fold, skip, gain)


def inner_grad_kernel(
    head_width,
    x_ref,
    dy_ref,
    b_ref,
    c_ref,
    decay_ref,
    source_ref,
    grown_ref,
    state_ref,
    dx_ref,
    dmeet_ref,
    dc_ref,
    meet_ref,
):
    rows = x_ref.shape[0]
    tiles = rows // LANES
    per_tile = LANES // head_width

    @pl.when(pl.program_id(0) == 0)
    def _():
        meet_ref[...] = against_cols(b_ref[...], c_ref[...])
        dmeet_ref[...] = jnp.zeros_like(dmeet_ref)
        dc_ref[...] = jnp.zeros_like(dc_ref)

    source_cols = source_ref[...].T
    grown_cols = grown_ref[...].T
    for early in range(tiles):
        in_rows = slice(early * LANES, (early + 1) * LANES)
        for late in range(early, tiles):
            out_rows = slice(late * LANES, (late + 1) * LANES)
            meet = meet_ref[in_rows, out_rows]
            total = dmeet_ref[in_rows, out_rows]
            for head in range(GROUP):
                lanes = slice(head * head_width, (head + 1) * head_width)
                weight = tile_exponent(
                    decay_ref[head : head + 1, out_rows],
                    source_cols[in_rows, head : head + 1],
                    early == late,
                    True,
                )
                dy = dy_ref[out_rows, lanes]
                high, low = halves(meet * weight)
                part = plain_dot(high, dy) + plain_dot(low, dy)
                if late == early:
                    dx_ref[in_rows, lanes] = part
                else:
                    dx_ref[in_rows, lanes] += part
                total = total + against_cols(x_ref[in_rows, lanes], dy) * weight
            dmeet_ref[in_rows, out_rows] = total
    for tile in range(x_ref.shape[1] // LANES):
        lanes = slice(tile * LANES, (tile + 1) * LANES)
        spread = per_head_lanes(grown_cols, tile * per_tile, head_width, rows)
        scaled = (dy_ref[:, lanes].astype(F32) * spread).astype(BF16)
        dc_ref[...] += against_cols(scaled, state_ref[:, lanes])


def inner_grad(x_rows, dy, b_rows, c_rows, decay, source, grown, state, head_width):
    rows, width = x_rows.shape
    states = b_rows.shape[1]
    block = GROUP * head_width
    group_rows = pl.BlockSpec((GROUP, rows), lambda g: (g, 0))
    return pl.pallas_call(
        functools.partial(inner_grad_kernel, head_width),
        out_shape=(
            jax.ShapeDtypeStruct((rows, width), F32),
            jax.ShapeDtypeStruct((rows, rows), F32),
            jax.ShapeDtypeStruct((rows, states), F32),
        ),
        grid=(width // block,),
        in_specs=[
            pl.BlockSpec((rows, block), lambda g: (0, g)),
            pl.BlockSpec((rows, block), lambda g: (0, g)),
            pl.BlockSpec((rows, states), lambda g: (0, 0)),
            pl.BlockSpec((rows, states), lambda g: (0, 0)),
            group_rows,
            group_rows,
            group_rows,
            pl.BlockSpec((states, block), lambda g: (0, g)),
        ],
        out_specs=(
            pl.BlockSpec((rows, block), lambda g: (0, g)),
            pl.BlockSpec((rows, rows), lambda g: (0, 0)),
            pl.BlockSpec((rows, states), lambda g: (0, 0)),
        ),
        scratch_shapes=[pltpu.VMEM((rows, rows), F32)],
        name="inner_grad",
    )(x_rows, dy, b_rows, c_rows, decay, source, grown, state)


def outer_grad_kernel(
    inner_ref,
    x_ref,
    dy_ref,
    b_ref,
    dstate_ref,
    toend_ref,
    spread_ref,
    fold_ref,
    skip_ref,
    dx_ref,
    colsum_ref,
    endsum_ref,
    db_ref,
):
    to_end = plain_dot(toend_ref[...], spread_ref[...])
    x_now = x_ref[...].astype(F32)
    through = to_end * plain_dot(b_ref[...], dstate_ref[...])
    d_scanned = inner_ref[...] + through
    dx_ref[...] = (d_scanned + skip_ref[...] * dy_ref[...].astype(F32)).astype(BF16)
    fold = fold_ref[...]
    high, low = halves(x_now * d_scanned)
    colsum_ref[...] = plain_dot(high, fold) + plain_dot(low, fold)
    high, low = halves(x_now * through)
    endsum_ref[...] = plain_dot(high, fold) + plain_dot(low, fold)
    db_ref[...] = against_cols((to_end * x_now).astype(BF16), dstate_ref[...])


def outer_grad(inner, x_rows, dy, b_rows, dstate, to_end, spread, fold, skip, row_block):
    rows, width = x_rows.shape
    states, heads = b_rows.shape[1], fold.shape[1]
    blocked = lambda cols: pl.BlockSpec((row_block, cols), lambda i: (i, 0))
    whole = lambda array: pl.BlockSpec(array.shape, lambda i: (0, 0))
    return pl.pallas_call(
        outer_grad_kernel,
        out_shape=(
            jax.ShapeDtypeStruct((rows, width), BF16),
            jax.ShapeDtypeStruct((rows, heads), F32),
            jax.ShapeDtypeStruct((rows, heads), F32),
            jax.ShapeDtypeStruct((rows, states), F32),
        ),
        grid=(rows // row_block,),
        in_specs=[
            blocked(width),
            blocked(width),
            blocked(width),
            blocked(states),
            whole(dstate),
            blocked(to_end.shape[1]),
            whole(spread),
            whole(fold),
            whole(skip),
        ],
        out_specs=(blocked(width), blocked(heads), blocked(heads), blocked(states)),
        name="outer_grad",
    )(inner, x_rows, dy, b_rows, dstate, to_end, spread, fold, skip)


def passed_along(value, axis, steps):
    count = lax.axis_size(axis)
    first, last = (max(0, -steps), min(count, count - steps))
    return lax.ppermute(value, axis, [(source, source + steps) for source in range(first, last)])


def three_parts(values):
    first = rounded(values)
    second = rounded(values - first)
    return first.astype(BF16), second.astype(BF16), (values - first - second).astype(BF16)


def carried_states(local, log_total, axis, backward, beside=None):
    count = lax.axis_size(axis)
    states, width = local.shape
    part = width // count
    wire = BF16 if backward or not WIDE else F32
    logs = three_parts(log_total) if wire == BF16 else (log_total,)
    packed = jnp.concatenate([local.astype(wire), *(p[None] for p in logs)], 0)
    split = packed.reshape(packed.shape[0], count, part).transpose(1, 0, 2)
    held = lax.all_to_all(split, axis, split_axis=0, concat_axis=0, tiled=True)
    if beside is not None:
        held = after(held, beside)
    own = held[:, :states].astype(F32)
    logs = jnp.sum(held[:, states:].astype(F32), axis=1)
    decay = jnp.exp(logs)
    order = range(count - 1, -1, -1) if backward else range(count)
    running = jnp.zeros((states, part), F32)
    entering = [None] * count
    for device in order:
        entering[device] = running.astype(wire)
        running = running * decay[device][None, :] + own[device]
    entering = jnp.stack(entering)
    return lax.all_to_all(entering, axis, split_axis=0, concat_axis=0, tiled=True), entering


def joined(home):
    count, states, part = home.shape
    return home.transpose(1, 0, 2).reshape(states, count * part)


def swapped(value, axis, mask):
    count = lax.axis_size(axis)
    return lax.ppermute(value, axis, [(source, source ^ mask) for source in range(count)])


def flip_order(count):
    order = [0]
    mask = count // 2
    while mask:
        order += [flip ^ mask for flip in order]
        mask //= 2
    return order


def gathered(value, axis):
    first = []
    mask = lax.axis_size(axis) // 2
    while mask:
        first.append(swapped(value, axis, mask))
        mask //= 2
    return value, first


def passed_on(started, axis, held_for=None):
    value, first = started
    if held_for is not None:
        first = after(first, held_for)
    blocks = [value]
    mask = lax.axis_size(axis) // 2
    for arrived in first:
        blocks += [arrived] + [swapped(block, axis, mask) for block in blocks[1:]]
        mask //= 2
    return blocks


def after(value, earlier):
    return lax.optimization_barrier((value, earlier))[0]


def weight_parts(shard, side):
    place = lax.axis_index(side) % 2
    rows = shard.shape[0]
    third = rows // 3 // 16 * 16
    alone = rows - 2 * third
    return (alone + place * third, 0, alone + (1 - place) * third), (third, alone, third)


def weight_sent(shard, axis, side):
    offsets, sizes = weight_parts(shard, side)
    shared, own = (
        lax.dynamic_slice_in_dim(shard, o, n, 0) for o, n in zip(offsets[:2], sizes[:2])
    )
    mask = lax.axis_size(axis) // 2
    if mask == 1:
        return (swapped(shard, axis, 1),)
    arrived = swapped(shared, axis, mask)
    direct = swapped(own, axis, mask)
    return swapped(shard, axis, 1), arrived, direct


def weight_gathered(shard, sent, axis, side):
    count, rank = lax.axis_size(axis), lax.axis_index(axis)
    rows = shard.shape[0]
    offsets, sizes = weight_parts(shard, side)
    held = {0: tuple(lax.dynamic_slice_in_dim(shard, o, n, 0) for o, n in zip(offsets, sizes))}
    whole = jnp.zeros((count * rows, shard.shape[1]), shard.dtype)
    mask = count // 2
    while mask > 1:
        for flip, (shared, own, _) in tuple(held.items()):
            if flip or mask < count // 2:
                arrived, direct = swapped(shared, axis, mask), swapped(own, axis, mask)
            else:
                arrived, direct = sent[1:]
            held[flip ^ mask] = (arrived, direct, swapped(arrived, side, 1))
        mask //= 2
    for flip, block in ((0, shard), (1, sent[0])):
        whole = lax.dynamic_update_slice_in_dim(whole, block, (rank ^ flip) * rows, 0)
    for flip, blocks in held.items():
        if flip:
            for block, offset in zip(blocks, offsets):
                start = (rank ^ flip) * rows + offset
                whole = lax.dynamic_update_slice_in_dim(whole, block, start, 0)
                start = (rank ^ flip ^ 1) * rows + offset
                whole = lax.dynamic_update_slice_in_dim(whole, swapped(block, axis, 1), start, 0)
    return whole


def exchanged(value, axis):
    count, rank = lax.axis_size(axis), lax.axis_index(axis)
    part = value.shape[1] // count
    blocks = []
    for flip in flip_order(count):
        piece = lax.dynamic_slice_in_dim(value, (rank ^ flip) * part, part, 1)
        blocks.append(swapped(piece, axis, flip) if flip else piece)
    return blocks


def product_kernel(place_ref, *refs):
    count = (len(refs) - 3) // 2
    left_refs, right_refs = refs[:count], refs[count : 2 * count]
    near_ref, away_ref, turned_ref = refs[2 * count :]
    tokens = left_refs[0].shape[0]

    @pl.when(pl.program_id(0) == 0)
    def _():
        for index, left_ref in enumerate(left_refs):
            turned_ref[:, index * tokens : (index + 1) * tokens] = left_ref[...].T

    half = near_ref.shape[0]
    for upper in range(2):
        rows = slice(upper * half, (upper + 1) * half)
        total = None
        for index, right_ref in enumerate(right_refs):
            part = plain_dot(
                turned_ref[rows, index * tokens : (index + 1) * tokens], right_ref[...]
            )
            total = part if total is None else total + part

        @pl.when(place_ref[0] == upper)
        def _():
            near_ref[...] = total

        @pl.when(place_ref[0] != upper)
        def _():
            away_ref[...] = total.astype(BF16)


def weight_product(lefts, rights, axis):
    place = (lax.axis_index(axis) % 2).astype(jnp.int32).reshape(1)
    tokens, rows = lefts[0].shape
    width = rights[0].shape[1]
    block = 512
    return pl.pallas_call(
        product_kernel,
        out_shape=(
            jax.ShapeDtypeStruct((rows // 2, width), F32),
            jax.ShapeDtypeStruct((rows // 2, width), BF16),
        ),
        grid_spec=pltpu.PrefetchScalarGridSpec(
            num_scalar_prefetch=1,
            grid=(pl.cdiv(width, block),),
            in_specs=[pl.BlockSpec((tokens, rows), lambda i, place: (0, 0)) for _ in lefts]
            + [pl.BlockSpec((tokens, block), lambda i, place: (0, i)) for _ in rights],
            out_specs=tuple(
                pl.BlockSpec((rows // 2, block), lambda i, place: (0, i)) for _ in range(2)
            ),
            scratch_shapes=[pltpu.VMEM((rows, tokens * len(lefts)), BF16)],
        ),
        name="weight_product",
    )(place, *lefts, *rights)


def seq_owned(near, arrived, axis):
    count, rank = lax.axis_size(axis), lax.axis_index(axis)
    line = rank // 2
    block = near.shape[0] // (count // 2)
    pair = near + arrived.astype(F32)
    total = lax.dynamic_slice_in_dim(pair, line * block, block, 0)
    for flip in range(1, count // 2):
        piece = lax.dynamic_slice_in_dim(pair, (line ^ flip) * block, block, 0).astype(BF16)
        total = total + swapped(piece, axis, 2 * flip).astype(F32)
    return total.astype(BF16)


def seq_spread(owned, axis):
    count = lax.axis_size(axis)
    blocks = [owned] + [swapped(owned, axis, 2 * flip) for flip in range(1, count // 2)]
    mine = jnp.stack(blocks)
    return mine, swapped(mine, axis, 1)


def place_kernel(ranks_ref, *refs):
    out_ref = refs[-1]
    count = pl.num_programs(0)
    mine = pl.program_id(0) // (count // 2) == ranks_ref[0]
    cursor = 0
    for pair in range(len(refs) // 2):
        near_ref, far_ref = refs[2 * pair], refs[2 * pair + 1]
        width = min(near_ref.shape[2], out_ref.shape[-1] - cursor)

        @pl.when(mine)
        def _():
            out_ref[..., cursor : cursor + width] = near_ref[:, :, :width].astype(F32).reshape(
                (*out_ref.shape[:-1], width)
            )

        @pl.when(jnp.logical_not(mine))
        def _():
            out_ref[..., cursor : cursor + width] = far_ref[:, :, :width].astype(F32).reshape(
                (*out_ref.shape[:-1], width)
            )

        cursor += width


def placed(spreads, axis, width):
    count, rank = lax.axis_size(axis), lax.axis_index(axis)
    ranks = jnp.stack([rank % 2, rank // 2]).astype(jnp.int32)
    flat = [array for pair in spreads for array in pair]
    rows = flat[0].shape[1]
    pick = lambda i, ranks: ((i % (count // 2)) ^ ranks[1], 0, 0)
    if rows % 8:
        shape, out_spec = (count, rows, width), pl.BlockSpec((1, rows, width), lambda i, r: (i, 0, 0))
    else:
        shape, out_spec = (count * rows, width), pl.BlockSpec((rows, width), lambda i, r: (i, 0))
    out = pl.pallas_call(
        place_kernel,
        out_shape=jax.ShapeDtypeStruct(shape, F32),
        grid_spec=pltpu.PrefetchScalarGridSpec(
            num_scalar_prefetch=1,
            grid=(count,),
            in_specs=[pl.BlockSpec((1, rows, a.shape[2]), pick) for a in flat],
            out_specs=out_spec,
        ),
        name="placed",
    )(ranks, *flat)
    return out.reshape(count * rows, width)


def turned_kernel(ranks_ref, near_a_ref, far_a_ref, near_b_ref, far_b_ref, out_ref, held_ref):
    line, rows = near_a_ref.shape[0], near_a_ref.shape[1]

    def fill(near_ref, far_ref):
        for index in range(2 * line):
            source = (index % line) ^ ranks_ref[1]
            mine = ranks_ref[0] == index // line
            block = jnp.where(mine, near_ref[source].astype(F32), far_ref[source].astype(F32))
            held_ref[index * rows : (index + 1) * rows, :] = block

    first = pl.program_id(0) < ranks_ref[2]

    @pl.when(first)
    def _():
        fill(near_a_ref, far_a_ref)

    @pl.when(jnp.logical_not(first))
    def _():
        fill(near_b_ref, far_b_ref)

    out_ref[...] = held_ref[...].T


def placed_turned(first, second, axis, width):
    count, rank = lax.axis_size(axis), lax.axis_index(axis)
    rows, columns = first[0].shape[1:]
    block = next(b for b in (512, 256, 128) if columns % b == 0)
    ahead = columns // block
    ranks = jnp.stack([rank % 2, rank // 2, ahead]).astype(jnp.int32)
    shape = (count // 2, rows, block)
    first_spec = pl.BlockSpec(shape, lambda j, r: (0, 0, jnp.minimum(j, ahead - 1)))
    second_spec = pl.BlockSpec(shape, lambda j, r: (0, 0, jnp.maximum(j - ahead, 0)))
    return pl.pallas_call(
        turned_kernel,
        out_shape=jax.ShapeDtypeStruct((width, count * rows), F32),
        grid_spec=pltpu.PrefetchScalarGridSpec(
            num_scalar_prefetch=1,
            grid=(pl.cdiv(width, block),),
            in_specs=[first_spec, first_spec, second_spec, second_spec],
            out_specs=pl.BlockSpec((block, count * rows), lambda j, r: (j, 0)),
            scratch_shapes=[pltpu.VMEM((count * rows, block), F32)],
        ),
        name="placed_turned",
    )(ranks, *first, *second).T


def small_total(packed, split_axis, axis):
    count, rank = lax.axis_size(split_axis), lax.axis_index(split_axis)
    total = None
    for flip in flip_order(count):
        row = lax.dynamic_slice_in_dim(packed, rank ^ flip, 1, 0)
        row = swapped(row, split_axis, flip) if flip else row
        total = row if total is None else total + row
    mask = lax.axis_size(axis) // 2
    while mask:
        total = total + swapped(total, axis, mask)
        mask //= 2
    return total[0]


def body(
    hidden,
    cotangent,
    norm_gain,
    in_weight,
    conv_weight,
    conv_bias,
    dt_bias,
    a_log,
    skip_d,
    inner_gain,
    out_weight,
):
    owner_count = lax.axis_size("fsdp")
    taps = conv_weight.shape[1]
    model = hidden.shape[2]
    inner_width = inner_gain.shape[0] * owner_count
    heads = a_log.shape[0] * owner_count
    conv_width = conv_bias.shape[0] * owner_count
    states = (conv_width - inner_width) // 2
    head_width = inner_width // heads
    tokens = hidden.shape[1]
    row_block = 64

    small = jnp.concatenate(
        [
            norm_gain,
            inner_gain,
            conv_bias,
            conv_weight.T.reshape(-1),
            dt_bias,
            a_log,
            skip_d,
        ]
    )
    small = jnp.pad(small, (0, -small.shape[0] % LANES))
    small_held = [swapped(small, "fsdp", flip) if flip else small for flip in range(owner_count)]
    small_held = jnp.stack(small_held)
    owner_rank = lax.axis_index("fsdp")
    small_all = jnp.concatenate(
        [
            lax.dynamic_slice_in_dim(small_held, owner_rank ^ owner, 1, 0)
            for owner in range(owner_count)
        ],
        0,
    )
    conv_shard, gate_shard = in_weight[:, inner_width:], in_weight[:, :inner_width]
    conv_sent = weight_sent(conv_shard, "fsdp", "seq")
    gate_sent = weight_sent(gate_shard, "fsdp", "seq")
    out_sent = weight_sent(out_weight, "fsdp", "seq")
    w_conv_in = weight_gathered(conv_shard, conv_sent, "fsdp", "seq")

    cursor = 0
    pieces = []
    for piece in (norm_gain, inner_gain, conv_bias, conv_weight, dt_bias, a_log, skip_d):
        pieces.append(small_all[:, cursor : cursor + piece.size].astype(F32))
        cursor += piece.size
    gain_n, gain_i, b_conv = (p.reshape(-1) for p in pieces[:3])
    w_taps = pieces[3].reshape(owner_count, taps, -1).transpose(1, 0, 2).reshape(taps, conv_width)
    bias_dt, log_a, skip_vec = (p.reshape(-1) for p in pieces[4:])

    hidden_f = hidden[0].astype(F32)
    cot_rows = cotangent[0]
    n_scale = lax.rsqrt(jnp.mean(hidden_f * hidden_f, axis=-1, keepdims=True) + EPS)
    n_unit = hidden_f * n_scale
    normed_b = (n_unit * gain_n).astype(BF16)

    stepped = plain_dot(normed_b, w_conv_in).astype(BF16)
    conv_in = stepped[:, :conv_width]
    raw_t = stepped[:, conv_width:].T.astype(F32)
    rim_rows = passed_along(conv_in[tokens - taps + 1 :], "seq", 1)
    gate_sent = after(gate_sent, rim_rows)
    w_gate = weight_gathered(gate_shard, gate_sent, "fsdp", "seq")
    padded = jnp.concatenate([rim_rows, conv_in], 0).astype(F32)
    pre_act = b_conv[None, :]
    for tap in range(taps):
        pre_act = pre_act + padded[tap : tap + tokens] * w_taps[tap]
    conv_act = jax.nn.silu(pre_act).astype(BF16)
    x_rows = conv_act[:, :inner_width]
    b_rows = conv_act[:, inner_width : inner_width + states]
    c_rows = conv_act[:, inner_width + states :]

    rate = -jnp.exp(log_a)[:, None]
    pre_step = raw_t + bias_dt[:, None]
    step = jax.nn.softplus(pre_step)
    ahead = jnp.triu(jnp.ones((tokens, tokens), F32))
    decay_log = jnp.dot(step * rate, ahead, precision=HIGHEST)
    source_log = decay_log - jnp.log(step)
    total_log = decay_log[:, -1]
    to_end = jnp.exp(total_log[:, None] - decay_log) * step
    grown = jnp.exp(decay_log)
    lane_head = jnp.arange(inner_width) // head_width
    one_hot = (jnp.arange(heads)[:, None] == lane_head[None, :]).astype(BF16)
    spread = jnp.concatenate([one_hot, one_hot], 0)
    fold = one_hot.T
    skip_lanes = jnp.repeat(skip_vec, head_width)[None, :]
    total_lanes = jnp.repeat(total_log, head_width)

    own_state = local_state(x_rows, b_rows.T, to_end, head_width)
    home, _ = carried_states(own_state, total_lanes, "seq", False)
    state_full = joined(home)
    state_in = host_halves(state_full)
    inner = inner_part(after(x_rows, own_state), b_rows, c_rows, decay_log, source_log, head_width)
    out_sent = after(out_sent, inner)
    w_out = weight_gathered(out_weight, out_sent, "fsdp", "seq")
    sent = out_sent[-1]
    gate_in = plain_dot(normed_b, w_gate).astype(BF16)
    d_gated = against_cols(cot_rows, w_out)

    gated_b, d_mixed, d_gate, own_dstate, rowsum, grad_gain_i, skip_sums = middle(
        inner,
        x_rows,
        gate_in,
        d_gated,
        c_rows,
        *state_in,
        jnp.concatenate(host_halves(grown.T), 1),
        spread,
        fold,
        skip_lanes,
        gain_i[None, :],
        row_block,
    )
    normed_all = exchanged(after(normed_b, sent), "fsdp")
    cot_all = gathered(after(cot_rows, sent), "fsdp")
    gated_all = exchanged(gated_b, "fsdp")
    d_gate_all = gathered(d_gate, "fsdp")
    inner_dx, d_meet, dc_carried = inner_grad(
        x_rows, d_mixed, b_rows, c_rows, decay_log, source_log, grown, state_in[0], head_width
    )
    home, _ = carried_states(own_dstate, total_lanes, "seq", True, inner_dx)
    cot_all = passed_on(cot_all, "fsdp")
    out_near, out_away = weight_product(gated_all, cot_all, "seq")
    out_arrived = swapped(out_away, "seq", 1)
    dstate = joined(after(home, out_near))
    d_x, colsum, endsum, db_carried = outer_grad(
        inner_dx,
        x_rows,
        d_mixed,
        b_rows,
        dstate,
        jnp.concatenate(host_halves(to_end.T), 1),
        spread,
        fold,
        skip_lanes,
        row_block,
    )
    out_arrived = after(out_arrived, d_x)
    d_gate_all = passed_on(d_gate_all, "fsdp", d_x)
    gate_near, gate_away = weight_product(normed_all, d_gate_all, "seq")
    gate_arrived = swapped(gate_away, "seq", 1)
    d_x = after(d_x, gate_near)
    d_meet_b = d_meet.astype(BF16)
    d_b = db_carried + plain_dot(d_meet_b, c_rows)
    d_c = dc_carried + across_rows(d_meet_b, b_rows)
    ends = jnp.sum(state_full * dstate.astype(F32), axis=0)
    ends = jnp.sum(ends.reshape(heads, head_width), axis=1) * jnp.exp(total_log)
    colsum_t = colsum.T
    d_log = rowsum.T - colsum_t
    d_last = jnp.sum(endsum, axis=0) + ends
    behind = jnp.tril(jnp.ones((tokens, tokens), F32))
    d_rate_step = jnp.dot(d_log, behind, precision=HIGHEST) + d_last[:, None]
    sig_step = jax.nn.sigmoid(pre_step)
    ratio = jnp.where(step > 0, sig_step / jnp.where(step > 0, step, 1.0), 0.0)
    d_raw = colsum_t * ratio + d_rate_step * rate * sig_step
    grad_log = jnp.sum(d_rate_step * step, axis=1) * rate[:, 0]
    grad_bias = jnp.sum(d_raw, axis=1)
    grad_skip = jnp.sum(skip_sums.reshape(heads, head_width), axis=1)

    d_conv = jnp.concatenate([d_x.astype(F32), d_b, d_c], 1)
    act_sig = jax.nn.sigmoid(pre_act)
    d_pre = d_conv * (act_sig * (1.0 + pre_act * (1.0 - act_sig)))
    after_rows = passed_along(d_pre[: taps - 1], "seq", -1)
    d_tail = jnp.concatenate([d_pre, after_rows], 0)
    d_conv_in = 0.0
    for tap in range(taps):
        shift = taps - 1 - tap
        d_conv_in = d_conv_in + d_tail[shift : shift + tokens] * w_taps[tap]
    spare = jnp.zeros((tokens, -(conv_width + heads) % LANES), BF16)
    d_step_proj = jnp.concatenate([d_conv_in.astype(BF16), d_raw.T.astype(BF16), spare], 1)
    block_out = hidden_f + plain_dot(after(gated_b, d_step_proj), w_out)
    d_step_all = passed_on(gathered(d_step_proj, "fsdp"), "fsdp", block_out)
    out_spread = seq_spread(seq_owned(out_near, out_arrived, "seq"), "seq")
    gate_arrived = after(gate_arrived, d_step_proj)
    gate_spread = seq_spread(seq_owned(gate_near, gate_arrived, "seq"), "seq")
    step_near, step_away = weight_product(normed_all, d_step_all, "seq")
    step_arrived = swapped(step_away, "seq", 1)
    step_spread = seq_spread(seq_owned(step_near, step_arrived, "seq"), "seq")
    d_pre = after(d_pre, d_step_proj)
    grad_w_conv = jnp.stack(
        [jnp.sum(d_pre * padded[tap : tap + tokens], axis=0) for tap in range(taps)]
    )
    grad_b_conv = jnp.sum(d_pre, axis=0)
    d_normed = against_cols(after(d_gate, d_step_proj), w_gate)
    d_normed = d_normed + against_cols(d_step_proj[:, : conv_width + heads], w_conv_in)
    d_unit = d_normed * gain_n
    d_hidden = n_scale * (d_unit - n_unit * jnp.mean(d_unit * n_unit, axis=-1, keepdims=True))
    grad_hidden = cot_rows.astype(F32) + d_hidden
    grad_gain_n = jnp.sum(d_normed * n_unit, axis=0)

    parts = (
        grad_gain_n,
        grad_gain_i[0],
        grad_b_conv,
        grad_bias,
        grad_log,
        grad_skip,
    )
    by_owner = [p.reshape(owner_count, -1) for p in parts]
    tap_part = grad_w_conv.reshape(taps, owner_count, -1).transpose(1, 0, 2)
    by_owner.append(tap_part.reshape(owner_count, -1))
    mine = small_total(jnp.concatenate(by_owner, 1), "fsdp", "seq")
    outs = []
    cursor = 0
    for part in by_owner:
        outs.append(mine[cursor : cursor + part.shape[1]])
        cursor += part.shape[1]
    return (
        block_out[None],
        grad_hidden[None],
        outs[0],
        placed_turned(gate_spread, step_spread, "seq", in_weight.shape[1]),
        outs[6].reshape(taps, -1).T,
        outs[2],
        outs[3],
        outs[4],
        outs[5],
        outs[1],
        placed((out_spread,), "seq", model),
    )


def solution(mesh):
    rows = P("fsdp", "seq", None)
    vector, matrix = P("fsdp"), P("fsdp", None)
    params = (vector, matrix, matrix, vector, vector, vector, vector, vector, matrix)
    return jax.shard_map(
        body,
        mesh=mesh,
        in_specs=(rows, rows, *params),
        out_specs=(rows, rows, *params),
        check_vma=False,
    )
```

```python
import functools

import jax
import jax.numpy as jnp
from jax import lax
from jax.experimental import pallas as pl
from jax.experimental.pallas import tpu as pltpu
from jax.sharding import PartitionSpec as P


EPS = 1e-05
LANES = 128
GROUP = 8
WIDE = True
BF16 = jnp.bfloat16
F32 = jnp.float32
HIGHEST = lax.Precision.HIGHEST


def dims(left, right, contract):
    return lax.dot_general(left, right, (contract, ((), ())), preferred_element_type=F32)


def across_rows(left, right):
    return dims(left, right, ((0,), (0,)))


def against_cols(left, right):
    return dims(left, right, ((1,), (1,)))


def plain_dot(left, right):
    return dims(left, right, ((1,), (0,)))


def halves(values):
    high = values.astype(BF16)
    return high, (values - high.astype(F32)).astype(BF16)


def rounded(values):
    return lax.reduce_precision(values, 8, 7)


def host_halves(values):
    high = rounded(values)
    return high.astype(BF16), (values - high).astype(BF16)


def per_head_lanes(columns, first, head_width, rows):
    per_tile = LANES // head_width
    lane = lax.broadcasted_iota(jnp.int32, (rows, LANES), 1)
    spread = jnp.broadcast_to(columns[:, first : first + 1], (rows, LANES))
    for extra in range(1, per_tile):
        column = columns[:, first + extra : first + extra + 1]
        spread = jnp.where(lane < extra * head_width, spread, column)
    return spread


def state_kernel(head_width, x_ref, bt_ref, te_ref, out_ref):
    rows = x_ref.shape[0]
    te_cols = te_ref[...].T
    per_tile = LANES // head_width
    for tile in range(x_ref.shape[1] // LANES):
        lanes = slice(tile * LANES, (tile + 1) * LANES)
        spread = per_head_lanes(te_cols, tile * per_tile, head_width, rows)
        high, low = halves(x_ref[:, lanes].astype(F32) * spread)
        out_ref[:, lanes] = plain_dot(bt_ref[...], high) + plain_dot(bt_ref[...], low)


def local_state(x_rows, b_cols, to_end, head_width):
    rows, width = x_rows.shape
    states = b_cols.shape[0]
    block = GROUP * head_width
    return pl.pallas_call(
        functools.partial(state_kernel, head_width),
        out_shape=jax.ShapeDtypeStruct((states, width), F32),
        grid=(width // block,),
        in_specs=[
            pl.BlockSpec((rows, block), lambda g: (0, g)),
            pl.BlockSpec((states, rows), lambda g: (0, 0)),
            pl.BlockSpec((GROUP, rows), lambda g: (g, 0)),
        ],
        out_specs=pl.BlockSpec((states, block), lambda g: (0, g)),
        name="local_state",
    )(x_rows, b_cols, to_end)


def tile_exponent(row_part, col_part, diagonal, lower):
    gap = row_part - col_part if lower else col_part - row_part
    if diagonal:
        first = lax.broadcasted_iota(jnp.int32, gap.shape, 0)
        second = lax.broadcasted_iota(jnp.int32, gap.shape, 1)
        keep = first >= second if not lower else second >= first
        gap = jnp.where(keep, gap, -1e30)
    return jnp.exp(gap)


def inner_kernel(head_width, x_ref, b_ref, c_ref, decay_ref, source_ref, out_ref, meet_ref):
    rows = x_ref.shape[0]
    tiles = rows // LANES

    @pl.when(pl.program_id(0) == 0)
    def _():
        meet_ref[...] = against_cols(c_ref[...], b_ref[...])

    decay_cols = decay_ref[...].T
    for late in range(tiles):
        out_rows = slice(late * LANES, (late + 1) * LANES)
        for head in range(GROUP):
            lanes = slice(head * head_width, (head + 1) * head_width)
            total = None
            for early in range(late + 1):
                in_rows = slice(early * LANES, (early + 1) * LANES)
                weight = tile_exponent(
                    source_ref[head : head + 1, in_rows],
                    decay_cols[out_rows, head : head + 1],
                    early == late,
                    False,
                )
                high, low = halves(meet_ref[out_rows, in_rows] * weight)
                x_now = x_ref[in_rows, lanes]
                part = plain_dot(high, x_now) + plain_dot(low, x_now)
                total = part if total is None else total + part
            out_ref[out_rows, lanes] = total


def inner_part(x_rows, b_rows, c_rows, decay, source, head_width):
    rows, width = x_rows.shape
    states = b_rows.shape[1]
    block = GROUP * head_width
    return pl.pallas_call(
        functools.partial(inner_kernel, head_width),
        out_shape=jax.ShapeDtypeStruct((rows, width), F32),
        grid=(width // block,),
        in_specs=[
            pl.BlockSpec((rows, block), lambda g: (0, g)),
            pl.BlockSpec((rows, states), lambda g: (0, 0)),
            pl.BlockSpec((rows, states), lambda g: (0, 0)),
            pl.BlockSpec((GROUP, rows), lambda g: (g, 0)),
            pl.BlockSpec((GROUP, rows), lambda g: (g, 0)),
        ],
        out_specs=pl.BlockSpec((rows, block), lambda g: (0, g)),
        scratch_shapes=[pltpu.VMEM((rows, rows), F32)],
        name="inner_part",
    )(x_rows, b_rows, c_rows, decay, source)


def middle_kernel(
    inner_ref,
    x_ref,
    gate_ref,
    dgated_ref,
    c_ref,
    state_ref,
    rest_ref,
    decay_ref,
    spread_ref,
    fold_ref,
    skip_ref,
    gain_ref,
    gated_ref,
    dmixed_ref,
    dgate_ref,
    dstate_ref,
    rowsum_ref,
    dgain_ref,
    dskip_ref,
):
    @pl.when(pl.program_id(0) == 0)
    def _():
        dstate_ref[...] = jnp.zeros_like(dstate_ref)
        dgain_ref[...] = jnp.zeros_like(dgain_ref)
        dskip_ref[...] = jnp.zeros_like(dskip_ref)

    decay = plain_dot(decay_ref[...], spread_ref[...])
    carried = plain_dot(c_ref[...], state_ref[...]) + plain_dot(c_ref[...], rest_ref[...])
    scanned = inner_ref[...] + carried * decay
    x_now = x_ref[...].astype(F32)
    mixed = (scanned + skip_ref[...] * x_now).astype(BF16).astype(F32)
    gate = gate_ref[...].astype(F32)
    sig = jax.nn.sigmoid(gate)
    act = gate * sig
    product = mixed * act
    scale = lax.rsqrt(jnp.mean(product * product, axis=-1, keepdims=True) + EPS)
    gain = gain_ref[...]
    unit = product * scale
    gated_ref[...] = (unit * gain).astype(BF16)
    d_gated = dgated_ref[...]
    dgain_ref[...] += jnp.sum(d_gated * unit, axis=0, keepdims=True)
    d_unit = d_gated * gain
    d_product = scale * (d_unit - unit * jnp.mean(d_unit * unit, axis=-1, keepdims=True))
    d_mixed_b = (d_product * act).astype(BF16)
    d_mixed = d_mixed_b.astype(F32)
    dmixed_ref[...] = d_mixed_b
    dgate_ref[...] = (d_product * mixed * (sig + act * (1.0 - sig))).astype(BF16)
    dskip_ref[...] += jnp.sum(d_mixed * x_now, axis=0, keepdims=True)
    high, low = halves(decay * d_mixed)
    dstate_ref[...] += across_rows(c_ref[...], high) + across_rows(c_ref[...], low)
    high, low = halves(d_mixed * scanned)
    rowsum_ref[...] = plain_dot(high, fold_ref[...]) + plain_dot(low, fold_ref[...])


def middle(inner, x_rows, gate, d_gated, c_rows, state, rest, decay, spread, fold, skip, gain, row_block):
    rows, width = x_rows.shape
    states, heads = c_rows.shape[1], fold.shape[1]
    blocked = lambda cols: pl.BlockSpec((row_block, cols), lambda i: (i, 0))
    whole = lambda array: pl.BlockSpec(array.shape, lambda i: (0, 0))
    kept = lambda *shape: pl.BlockSpec(shape, lambda i: (0, 0))
    return pl.pallas_call(
        middle_kernel,
        out_shape=(
            jax.ShapeDtypeStruct((rows, width), BF16),
            jax.ShapeDtypeStruct((rows, width), BF16),
            jax.ShapeDtypeStruct((rows, width), BF16),
            jax.ShapeDtypeStruct((states, width), F32),
            jax.ShapeDtypeStruct((rows, heads), F32),
            jax.ShapeDtypeStruct((1, width), F32),
            jax.ShapeDtypeStruct((1, width), F32),
        ),
        grid=(rows // row_block,),
        in_specs=[
            blocked(width),
            blocked(width),
            blocked(width),
            blocked(width),
            blocked(states),
            whole(state),
            whole(rest),
            blocked(decay.shape[1]),
            whole(spread),
            whole(fold),
            whole(skip),
            whole(gain),
        ],
        out_specs=(
            blocked(width),
            blocked(width),
            blocked(width),
            kept(states, width),
            blocked(heads),
            kept(1, width),
            kept(1, width),
        ),
        name="middle",
    )(inner, x_rows, gate, d_gated, c_rows, state, rest, decay, spread, fold, skip, gain)


def inner_grad_kernel(
    head_width,
    x_ref,
    dy_ref,
    b_ref,
    c_ref,
    decay_ref,
    source_ref,
    grown_ref,
    state_ref,
    dx_ref,
    dmeet_ref,
    dc_ref,
    meet_ref,
):
    rows = x_ref.shape[0]
    tiles = rows // LANES
    per_tile = LANES // head_width

    @pl.when(pl.program_id(0) == 0)
    def _():
        meet_ref[...] = against_cols(b_ref[...], c_ref[...])
        dmeet_ref[...] = jnp.zeros_like(dmeet_ref)
        dc_ref[...] = jnp.zeros_like(dc_ref)

    source_cols = source_ref[...].T
    grown_cols = grown_ref[...].T
    for early in range(tiles):
        in_rows = slice(early * LANES, (early + 1) * LANES)
        for late in range(early, tiles):
            out_rows = slice(late * LANES, (late + 1) * LANES)
            meet = meet_ref[in_rows, out_rows]
            total = dmeet_ref[in_rows, out_rows]
            for head in range(GROUP):
                lanes = slice(head * head_width, (head + 1) * head_width)
                weight = tile_exponent(
                    decay_ref[head : head + 1, out_rows],
                    source_cols[in_rows, head : head + 1],
                    early == late,
                    True,
                )
                dy = dy_ref[out_rows, lanes]
                high, low = halves(meet * weight)
                part = plain_dot(high, dy) + plain_dot(low, dy)
                if late == early:
                    dx_ref[in_rows, lanes] = part
                else:
                    dx_ref[in_rows, lanes] += part
                total = total + against_cols(x_ref[in_rows, lanes], dy) * weight
            dmeet_ref[in_rows, out_rows] = total
    for tile in range(x_ref.shape[1] // LANES):
        lanes = slice(tile * LANES, (tile + 1) * LANES)
        spread = per_head_lanes(grown_cols, tile * per_tile, head_width, rows)
        scaled = (dy_ref[:, lanes].astype(F32) * spread).astype(BF16)
        dc_ref[...] += against_cols(scaled, state_ref[:, lanes])


def inner_grad(x_rows, dy, b_rows, c_rows, decay, source, grown, state, head_width):
    rows, width = x_rows.shape
    states = b_rows.shape[1]
    block = GROUP * head_width
    group_rows = pl.BlockSpec((GROUP, rows), lambda g: (g, 0))
    return pl.pallas_call(
        functools.partial(inner_grad_kernel, head_width),
        out_shape=(
            jax.ShapeDtypeStruct((rows, width), F32),
            jax.ShapeDtypeStruct((rows, rows), F32),
            jax.ShapeDtypeStruct((rows, states), F32),
        ),
        grid=(width // block,),
        in_specs=[
            pl.BlockSpec((rows, block), lambda g: (0, g)),
            pl.BlockSpec((rows, block), lambda g: (0, g)),
            pl.BlockSpec((rows, states), lambda g: (0, 0)),
            pl.BlockSpec((rows, states), lambda g: (0, 0)),
            group_rows,
            group_rows,
            group_rows,
            pl.BlockSpec((states, block), lambda g: (0, g)),
        ],
        out_specs=(
            pl.BlockSpec((rows, block), lambda g: (0, g)),
            pl.BlockSpec((rows, rows), lambda g: (0, 0)),
            pl.BlockSpec((rows, states), lambda g: (0, 0)),
        ),
        scratch_shapes=[pltpu.VMEM((rows, rows), F32)],
        name="inner_grad",
    )(x_rows, dy, b_rows, c_rows, decay, source, grown, state)


def outer_grad_kernel(
    inner_ref,
    x_ref,
    dy_ref,
    b_ref,
    dstate_ref,
    toend_ref,
    spread_ref,
    fold_ref,
    skip_ref,
    dx_ref,
    colsum_ref,
    endsum_ref,
    db_ref,
):
    to_end = plain_dot(toend_ref[...], spread_ref[...])
    x_now = x_ref[...].astype(F32)
    through = to_end * plain_dot(b_ref[...], dstate_ref[...])
    d_scanned = inner_ref[...] + through
    dx_ref[...] = (d_scanned + skip_ref[...] * dy_ref[...].astype(F32)).astype(BF16)
    fold = fold_ref[...]
    high, low = halves(x_now * d_scanned)
    colsum_ref[...] = plain_dot(high, fold) + plain_dot(low, fold)
    high, low = halves(x_now * through)
    endsum_ref[...] = plain_dot(high, fold) + plain_dot(low, fold)
    db_ref[...] = against_cols((to_end * x_now).astype(BF16), dstate_ref[...])


def outer_grad(inner, x_rows, dy, b_rows, dstate, to_end, spread, fold, skip, row_block):
    rows, width = x_rows.shape
    states, heads = b_rows.shape[1], fold.shape[1]
    blocked = lambda cols: pl.BlockSpec((row_block, cols), lambda i: (i, 0))
    whole = lambda array: pl.BlockSpec(array.shape, lambda i: (0, 0))
    return pl.pallas_call(
        outer_grad_kernel,
        out_shape=(
            jax.ShapeDtypeStruct((rows, width), BF16),
            jax.ShapeDtypeStruct((rows, heads), F32),
            jax.ShapeDtypeStruct((rows, heads), F32),
            jax.ShapeDtypeStruct((rows, states), F32),
        ),
        grid=(rows // row_block,),
        in_specs=[
            blocked(width),
            blocked(width),
            blocked(width),
            blocked(states),
            whole(dstate),
            blocked(to_end.shape[1]),
            whole(spread),
            whole(fold),
            whole(skip),
        ],
        out_specs=(blocked(width), blocked(heads), blocked(heads), blocked(states)),
        name="outer_grad",
    )(inner, x_rows, dy, b_rows, dstate, to_end, spread, fold, skip)


def passed_along(value, axis, steps):
    count = lax.axis_size(axis)
    first, last = (max(0, -steps), min(count, count - steps))
    return lax.ppermute(value, axis, [(source, source + steps) for source in range(first, last)])


def three_parts(values):
    first = rounded(values)
    second = rounded(values - first)
    return first.astype(BF16), second.astype(BF16), (values - first - second).astype(BF16)


def carried_states(local, log_total, axis, backward, beside=None):
    count = lax.axis_size(axis)
    states, width = local.shape
    part = width // count
    wire = BF16 if backward or not WIDE else F32
    logs = three_parts(log_total) if wire == BF16 else (log_total,)
    packed = jnp.concatenate([local.astype(wire), *(p[None] for p in logs)], 0)
    split = packed.reshape(packed.shape[0], count, part).transpose(1, 0, 2)
    held = lax.all_to_all(split, axis, split_axis=0, concat_axis=0, tiled=True)
    if beside is not None:
        held = after(held, beside)
    own = held[:, :states].astype(F32)
    logs = jnp.sum(held[:, states:].astype(F32), axis=1)
    decay = jnp.exp(logs)
    order = range(count - 1, -1, -1) if backward else range(count)
    running = jnp.zeros((states, part), F32)
    entering = [None] * count
    for device in order:
        entering[device] = running.astype(wire)
        running = running * decay[device][None, :] + own[device]
    entering = jnp.stack(entering)
    return lax.all_to_all(entering, axis, split_axis=0, concat_axis=0, tiled=True), entering


def joined(home):
    count, states, part = home.shape
    return home.transpose(1, 0, 2).reshape(states, count * part)


def swapped(value, axis, mask):
    count = lax.axis_size(axis)
    return lax.ppermute(value, axis, [(source, source ^ mask) for source in range(count)])


def flip_order(count):
    order = [0]
    mask = count // 2
    while mask:
        order += [flip ^ mask for flip in order]
        mask //= 2
    return order


def gathered(value, axis):
    first = []
    mask = lax.axis_size(axis) // 2
    while mask:
        first.append(swapped(value, axis, mask))
        mask //= 2
    return value, first


def passed_on(started, axis, held_for=None):
    value, first = started
    if held_for is not None:
        first = after(first, held_for)
    blocks = [value]
    mask = lax.axis_size(axis) // 2
    for arrived in first:
        blocks += [arrived] + [swapped(block, axis, mask) for block in blocks[1:]]
        mask //= 2
    return blocks


def after(value, earlier):
    return lax.optimization_barrier((value, earlier))[0]


def weight_parts(shard, side):
    place = lax.axis_index(side) % 2
    rows = shard.shape[0]
    third = rows // 3 // 16 * 16
    alone = rows - 2 * third
    return (alone + place * third, 0, alone + (1 - place) * third), (third, alone, third)


def weight_sent(shard, axis, side):
    offsets, sizes = weight_parts(shard, side)
    shared, own = (
        lax.dynamic_slice_in_dim(shard, o, n, 0) for o, n in zip(offsets[:2], sizes[:2])
    )
    mask = lax.axis_size(axis) // 2
    if mask == 1:
        return (swapped(shard, axis, 1),)
    arrived = swapped(shared, axis, mask)
    direct = swapped(own, axis, mask)
    return swapped(shard, axis, 1), arrived, direct


def weight_gathered(shard, sent, axis, side, earlier=None):
    held_for = (lambda block: block) if earlier is None else (lambda block: after(block, earlier))
    count, rank = lax.axis_size(axis), lax.axis_index(axis)
    rows = shard.shape[0]
    offsets, sizes = weight_parts(shard, side)
    held = {0: tuple(lax.dynamic_slice_in_dim(shard, o, n, 0) for o, n in zip(offsets, sizes))}
    whole = jnp.zeros((count * rows, shard.shape[1]), shard.dtype)
    mask = count // 2
    while mask > 1:
        for flip, (shared, own, _) in tuple(held.items()):
            if flip or mask < count // 2:
                arrived, direct = swapped(shared, axis, mask), swapped(own, axis, mask)
            else:
                arrived, direct = sent[1:]
            held[flip ^ mask] = (arrived, direct, swapped(arrived, side, 1))
        mask //= 2
    for flip, block in ((0, shard), (1, sent[0])):
        whole = lax.dynamic_update_slice_in_dim(whole, held_for(block), (rank ^ flip) * rows, 0)
    for flip, blocks in held.items():
        if flip:
            for block, offset in zip(blocks, offsets):
                start = (rank ^ flip) * rows + offset
                near = swapped(block, axis, 1)
                whole = lax.dynamic_update_slice_in_dim(whole, held_for(block), start, 0)
                start = (rank ^ flip ^ 1) * rows + offset
                whole = lax.dynamic_update_slice_in_dim(whole, held_for(near), start, 0)
    return whole


def exchanged(value, axis):
    count, rank = lax.axis_size(axis), lax.axis_index(axis)
    part = value.shape[1] // count
    blocks = []
    for flip in flip_order(count):
        piece = lax.dynamic_slice_in_dim(value, (rank ^ flip) * part, part, 1)
        blocks.append(swapped(piece, axis, flip) if flip else piece)
    return blocks


def product_kernel(place_ref, *refs):
    count = (len(refs) - 3) // 2
    left_refs, right_refs = refs[:count], refs[count : 2 * count]
    near_ref, away_ref, turned_ref = refs[2 * count :]
    tokens = left_refs[0].shape[0]

    @pl.when(pl.program_id(0) == 0)
    def _():
        for index, left_ref in enumerate(left_refs):
            turned_ref[:, index * tokens : (index + 1) * tokens] = left_ref[...].T

    half = near_ref.shape[0]
    for upper in range(2):
        rows = slice(upper * half, (upper + 1) * half)
        total = None
        for index, right_ref in enumerate(right_refs):
            part = plain_dot(
                turned_ref[rows, index * tokens : (index + 1) * tokens], right_ref[...]
            )
            total = part if total is None else total + part

        @pl.when(place_ref[0] == upper)
        def _():
            near_ref[...] = total

        @pl.when(place_ref[0] != upper)
        def _():
            away_ref[...] = total.astype(BF16)


def weight_product(lefts, rights, axis):
    place = (lax.axis_index(axis) % 2).astype(jnp.int32).reshape(1)
    tokens, rows = lefts[0].shape
    width = rights[0].shape[1]
    block = 512
    return pl.pallas_call(
        product_kernel,
        out_shape=(
            jax.ShapeDtypeStruct((rows // 2, width), F32),
            jax.ShapeDtypeStruct((rows // 2, width), BF16),
        ),
        grid_spec=pltpu.PrefetchScalarGridSpec(
            num_scalar_prefetch=1,
            grid=(pl.cdiv(width, block),),
            in_specs=[pl.BlockSpec((tokens, rows), lambda i, place: (0, 0)) for _ in lefts]
            + [pl.BlockSpec((tokens, block), lambda i, place: (0, i)) for _ in rights],
            out_specs=tuple(
                pl.BlockSpec((rows // 2, block), lambda i, place: (0, i)) for _ in range(2)
            ),
            scratch_shapes=[pltpu.VMEM((rows, tokens * len(lefts)), BF16)],
        ),
        name="weight_product",
    )(place, *lefts, *rights)


def seq_owned(near, arrived, axis):
    count, rank = lax.axis_size(axis), lax.axis_index(axis)
    line = rank // 2
    block = near.shape[0] // (count // 2)
    pair = near + arrived.astype(F32)
    total = lax.dynamic_slice_in_dim(pair, line * block, block, 0)
    for flip in range(1, count // 2):
        piece = lax.dynamic_slice_in_dim(pair, (line ^ flip) * block, block, 0).astype(BF16)
        total = total + swapped(piece, axis, 2 * flip).astype(F32)
    return total.astype(BF16)


def seq_spread(owned, axis):
    count = lax.axis_size(axis)
    blocks = [owned] + [swapped(owned, axis, 2 * flip) for flip in range(1, count // 2)]
    mine = jnp.stack(blocks)
    return mine, swapped(mine, axis, 1)


def place_kernel(ranks_ref, *refs):
    out_ref = refs[-1]
    count = pl.num_programs(0)
    mine = pl.program_id(0) // (count // 2) == ranks_ref[0]
    cursor = 0
    for pair in range(len(refs) // 2):
        near_ref, far_ref = refs[2 * pair], refs[2 * pair + 1]
        width = min(near_ref.shape[2], out_ref.shape[-1] - cursor)

        @pl.when(mine)
        def _():
            out_ref[..., cursor : cursor + width] = near_ref[:, :, :width].astype(F32).reshape(
                (*out_ref.shape[:-1], width)
            )

        @pl.when(jnp.logical_not(mine))
        def _():
            out_ref[..., cursor : cursor + width] = far_ref[:, :, :width].astype(F32).reshape(
                (*out_ref.shape[:-1], width)
            )

        cursor += width


def placed(spreads, axis, width):
    count, rank = lax.axis_size(axis), lax.axis_index(axis)
    ranks = jnp.stack([rank % 2, rank // 2]).astype(jnp.int32)
    flat = [array for pair in spreads for array in pair]
    rows = flat[0].shape[1]
    pick = lambda i, ranks: ((i % (count // 2)) ^ ranks[1], 0, 0)
    if rows % 8:
        shape, out_spec = (count, rows, width), pl.BlockSpec((1, rows, width), lambda i, r: (i, 0, 0))
    else:
        shape, out_spec = (count * rows, width), pl.BlockSpec((rows, width), lambda i, r: (i, 0))
    out = pl.pallas_call(
        place_kernel,
        out_shape=jax.ShapeDtypeStruct(shape, F32),
        grid_spec=pltpu.PrefetchScalarGridSpec(
            num_scalar_prefetch=1,
            grid=(count,),
            in_specs=[pl.BlockSpec((1, rows, a.shape[2]), pick) for a in flat],
            out_specs=out_spec,
        ),
        name="placed",
    )(ranks, *flat)
    return out.reshape(count * rows, width)


def turned_kernel(ranks_ref, near_a_ref, far_a_ref, near_b_ref, far_b_ref, out_ref, held_ref):
    line, rows = near_a_ref.shape[0], near_a_ref.shape[1]

    def fill(near_ref, far_ref):
        for index in range(2 * line):
            source = (index % line) ^ ranks_ref[1]
            mine = ranks_ref[0] == index // line
            block = jnp.where(mine, near_ref[source].astype(F32), far_ref[source].astype(F32))
            held_ref[index * rows : (index + 1) * rows, :] = block

    first = pl.program_id(0) < ranks_ref[2]

    @pl.when(first)
    def _():
        fill(near_a_ref, far_a_ref)

    @pl.when(jnp.logical_not(first))
    def _():
        fill(near_b_ref, far_b_ref)

    out_ref[...] = held_ref[...].T


def placed_turned(first, second, axis, width):
    count, rank = lax.axis_size(axis), lax.axis_index(axis)
    rows, columns = first[0].shape[1:]
    block = next(b for b in (512, 256, 128) if columns % b == 0)
    ahead = columns // block
    ranks = jnp.stack([rank % 2, rank // 2, ahead]).astype(jnp.int32)
    shape = (count // 2, rows, block)
    first_spec = pl.BlockSpec(shape, lambda j, r: (0, 0, jnp.minimum(j, ahead - 1)))
    second_spec = pl.BlockSpec(shape, lambda j, r: (0, 0, jnp.maximum(j - ahead, 0)))
    return pl.pallas_call(
        turned_kernel,
        out_shape=jax.ShapeDtypeStruct((width, count * rows), F32),
        grid_spec=pltpu.PrefetchScalarGridSpec(
            num_scalar_prefetch=1,
            grid=(pl.cdiv(width, block),),
            in_specs=[first_spec, first_spec, second_spec, second_spec],
            out_specs=pl.BlockSpec((block, count * rows), lambda j, r: (j, 0)),
            scratch_shapes=[pltpu.VMEM((count * rows, block), F32)],
        ),
        name="placed_turned",
    )(ranks, *first, *second).T


def small_total(packed, split_axis, axis):
    count, rank = lax.axis_size(split_axis), lax.axis_index(split_axis)
    total = None
    for flip in flip_order(count):
        row = lax.dynamic_slice_in_dim(packed, rank ^ flip, 1, 0)
        row = swapped(row, split_axis, flip) if flip else row
        total = row if total is None else total + row
    mask = lax.axis_size(axis) // 2
    while mask:
        total = total + swapped(total, axis, mask)
        mask //= 2
    return total[0]


def body(
    hidden,
    cotangent,
    norm_gain,
    in_weight,
    conv_weight,
    conv_bias,
    dt_bias,
    a_log,
    skip_d,
    inner_gain,
    out_weight,
):
    owner_count = lax.axis_size("fsdp")
    taps = conv_weight.shape[1]
    model = hidden.shape[2]
    inner_width = inner_gain.shape[0] * owner_count
    heads = a_log.shape[0] * owner_count
    conv_width = conv_bias.shape[0] * owner_count
    states = (conv_width - inner_width) // 2
    head_width = inner_width // heads
    tokens = hidden.shape[1]
    row_block = 64

    small = jnp.concatenate(
        [
            norm_gain,
            inner_gain,
            conv_bias,
            conv_weight.T.reshape(-1),
            dt_bias,
            a_log,
            skip_d,
        ]
    )
    small = jnp.pad(small, (0, -small.shape[0] % LANES))
    small_held = [swapped(small, "fsdp", flip) if flip else small for flip in range(owner_count)]
    small_held = jnp.stack(small_held)
    owner_rank = lax.axis_index("fsdp")
    small_all = jnp.concatenate(
        [
            lax.dynamic_slice_in_dim(small_held, owner_rank ^ owner, 1, 0)
            for owner in range(owner_count)
        ],
        0,
    )
    conv_shard, gate_shard = in_weight[:, inner_width:], in_weight[:, :inner_width]
    conv_sent = weight_sent(conv_shard, "fsdp", "seq")
    gate_sent = weight_sent(gate_shard, "fsdp", "seq")
    out_sent = weight_sent(out_weight, "fsdp", "seq")
    w_conv_in = weight_gathered(conv_shard, conv_sent, "fsdp", "seq")

    cursor = 0
    pieces = []
    for piece in (norm_gain, inner_gain, conv_bias, conv_weight, dt_bias, a_log, skip_d):
        pieces.append(small_all[:, cursor : cursor + piece.size].astype(F32))
        cursor += piece.size
    gain_n, gain_i, b_conv = (p.reshape(-1) for p in pieces[:3])
    w_taps = pieces[3].reshape(owner_count, taps, -1).transpose(1, 0, 2).reshape(taps, conv_width)
    bias_dt, log_a, skip_vec = (p.reshape(-1) for p in pieces[4:])

    hidden_f = hidden[0].astype(F32)
    cot_rows = cotangent[0]
    n_scale = lax.rsqrt(jnp.mean(hidden_f * hidden_f, axis=-1, keepdims=True) + EPS)
    n_unit = hidden_f * n_scale
    normed_b = (n_unit * gain_n).astype(BF16)

    stepped = plain_dot(normed_b, w_conv_in).astype(BF16)
    conv_in = stepped[:, :conv_width]
    raw_t = stepped[:, conv_width:].T.astype(F32)
    rim_rows = passed_along(conv_in[tokens - taps + 1 :], "seq", 1)
    gate_sent = after(gate_sent, rim_rows)
    padded = jnp.concatenate([rim_rows, conv_in], 0).astype(F32)
    pre_act = b_conv[None, :]
    for tap in range(taps):
        pre_act = pre_act + padded[tap : tap + tokens] * w_taps[tap]
    conv_act = jax.nn.silu(pre_act).astype(BF16)
    x_rows = conv_act[:, :inner_width]
    b_rows = conv_act[:, inner_width : inner_width + states]
    c_rows = conv_act[:, inner_width + states :]

    rate = -jnp.exp(log_a)[:, None]
    pre_step = raw_t + bias_dt[:, None]
    step = jax.nn.softplus(pre_step)
    ahead = jnp.triu(jnp.ones((tokens, tokens), F32))
    decay_log = jnp.dot(step * rate, ahead, precision=HIGHEST)
    source_log = decay_log - jnp.log(step)
    total_log = decay_log[:, -1]
    to_end = jnp.exp(total_log[:, None] - decay_log) * step
    grown = jnp.exp(decay_log)
    lane_head = jnp.arange(inner_width) // head_width
    one_hot = (jnp.arange(heads)[:, None] == lane_head[None, :]).astype(BF16)
    spread = jnp.concatenate([one_hot, one_hot], 0)
    fold = one_hot.T
    skip_lanes = jnp.repeat(skip_vec, head_width)[None, :]
    total_lanes = jnp.repeat(total_log, head_width)

    own_state = local_state(x_rows, b_rows.T, to_end, head_width)
    home, entering = carried_states(own_state, total_lanes, "seq", False)
    state_full = joined(home)
    state_in = host_halves(state_full)
    inner = inner_part(after(x_rows, own_state), b_rows, c_rows, decay_log, source_log, head_width)
    out_sent = after(out_sent, (inner, entering))
    w_gate = weight_gathered(gate_shard, gate_sent, "fsdp", "seq", entering)
    w_out = weight_gathered(out_weight, out_sent, "fsdp", "seq")
    sent = out_sent[-1]
    gate_in = plain_dot(normed_b, w_gate).astype(BF16)
    d_gated = against_cols(cot_rows, w_out)

    gated_b, d_mixed, d_gate, own_dstate, rowsum, grad_gain_i, skip_sums = middle(
        inner,
        x_rows,
        gate_in,
        d_gated,
        c_rows,
        *state_in,
        jnp.concatenate(host_halves(grown.T), 1),
        spread,
        fold,
        skip_lanes,
        gain_i[None, :],
        row_block,
    )
    normed_all = exchanged(after(normed_b, sent), "fsdp")
    cot_all = gathered(after(cot_rows, sent), "fsdp")
    gated_all = exchanged(gated_b, "fsdp")
    d_gate_all = gathered(d_gate, "fsdp")
    inner_dx, d_meet, dc_carried = inner_grad(
        x_rows, d_mixed, b_rows, c_rows, decay_log, source_log, grown, state_in[0], head_width
    )
    home, _ = carried_states(own_dstate, total_lanes, "seq", True, inner_dx)
    cot_all = passed_on(cot_all, "fsdp")
    out_near, out_away = weight_product(gated_all, cot_all, "seq")
    out_arrived = swapped(out_away, "seq", 1)
    dstate = joined(after(home, out_near))
    d_x, colsum, endsum, db_carried = outer_grad(
        inner_dx,
        x_rows,
        d_mixed,
        b_rows,
        dstate,
        jnp.concatenate(host_halves(to_end.T), 1),
        spread,
        fold,
        skip_lanes,
        row_block,
    )
    out_arrived = after(out_arrived, d_x)
    d_gate_all = passed_on(d_gate_all, "fsdp", d_x)
    gate_near, gate_away = weight_product(normed_all, d_gate_all, "seq")
    gate_arrived = swapped(gate_away, "seq", 1)
    d_x = after(d_x, gate_near)
    d_meet_b = d_meet.astype(BF16)
    d_b = db_carried + plain_dot(d_meet_b, c_rows)
    d_c = dc_carried + across_rows(d_meet_b, b_rows)
    ends = jnp.sum(state_full * dstate.astype(F32), axis=0)
    ends = jnp.sum(ends.reshape(heads, head_width), axis=1) * jnp.exp(total_log)
    colsum_t = colsum.T
    d_log = rowsum.T - colsum_t
    d_last = jnp.sum(endsum, axis=0) + ends
    behind = jnp.tril(jnp.ones((tokens, tokens), F32))
    d_rate_step = jnp.dot(d_log, behind, precision=HIGHEST) + d_last[:, None]
    sig_step = jax.nn.sigmoid(pre_step)
    ratio = jnp.where(step > 0, sig_step / jnp.where(step > 0, step, 1.0), 0.0)
    d_raw = colsum_t * ratio + d_rate_step * rate * sig_step
    grad_log = jnp.sum(d_rate_step * step, axis=1) * rate[:, 0]
    grad_bias = jnp.sum(d_raw, axis=1)
    grad_skip = jnp.sum(skip_sums.reshape(heads, head_width), axis=1)

    d_conv = jnp.concatenate([d_x.astype(F32), d_b, d_c], 1)
    act_sig = jax.nn.sigmoid(pre_act)
    d_pre = d_conv * (act_sig * (1.0 + pre_act * (1.0 - act_sig)))
    after_rows = passed_along(d_pre[: taps - 1], "seq", -1)
    d_tail = jnp.concatenate([d_pre, after_rows], 0)
    d_conv_in = 0.0
    for tap in range(taps):
        shift = taps - 1 - tap
        d_conv_in = d_conv_in + d_tail[shift : shift + tokens] * w_taps[tap]
    spare = jnp.zeros((tokens, -(conv_width + heads) % LANES), BF16)
    d_step_proj = jnp.concatenate([d_conv_in.astype(BF16), d_raw.T.astype(BF16), spare], 1)
    block_out = hidden_f + plain_dot(after(gated_b, d_step_proj), w_out)
    d_pre = after(d_pre, d_step_proj)
    grad_w_conv = jnp.stack(
        [jnp.sum(d_pre * padded[tap : tap + tokens], axis=0) for tap in range(taps)]
    )
    grad_b_conv = jnp.sum(d_pre, axis=0)
    d_step_all = passed_on(
        gathered(d_step_proj, "fsdp"), "fsdp", (block_out, grad_w_conv, grad_b_conv)
    )
    out_spread = seq_spread(seq_owned(out_near, out_arrived, "seq"), "seq")
    gate_arrived = after(gate_arrived, d_step_proj)
    gate_spread = seq_spread(seq_owned(gate_near, gate_arrived, "seq"), "seq")
    step_near, step_away = weight_product(normed_all, d_step_all, "seq")
    step_arrived = swapped(step_away, "seq", 1)
    step_spread = seq_spread(seq_owned(step_near, step_arrived, "seq"), "seq")
    d_normed = against_cols(after(d_gate, d_step_proj), w_gate)
    d_normed = d_normed + against_cols(d_step_proj[:, : conv_width + heads], w_conv_in)
    d_unit = d_normed * gain_n
    d_hidden = n_scale * (d_unit - n_unit * jnp.mean(d_unit * n_unit, axis=-1, keepdims=True))
    grad_hidden = cot_rows.astype(F32) + d_hidden
    grad_gain_n = jnp.sum(d_normed * n_unit, axis=0)

    parts = (
        grad_gain_n,
        grad_gain_i[0],
        grad_b_conv,
        grad_bias,
        grad_log,
        grad_skip,
    )
    by_owner = [p.reshape(owner_count, -1) for p in parts]
    tap_part = grad_w_conv.reshape(taps, owner_count, -1).transpose(1, 0, 2)
    by_owner.append(tap_part.reshape(owner_count, -1))
    mine = small_total(jnp.concatenate(by_owner, 1), "fsdp", "seq")
    outs = []
    cursor = 0
    for part in by_owner:
        outs.append(mine[cursor : cursor + part.shape[1]])
        cursor += part.shape[1]
    grad_w_out = placed((out_spread,), "seq", model)
    return (
        block_out[None],
        grad_hidden[None],
        outs[0],
        placed_turned(gate_spread, step_spread, "seq", in_weight.shape[1]),
        outs[6].reshape(taps, -1).T,
        outs[2],
        outs[3],
        outs[4],
        outs[5],
        outs[1],
        grad_w_out,
    )


def solution(mesh):
    rows = P("fsdp", "seq", None)
    vector, matrix = P("fsdp"), P("fsdp", None)
    params = (vector, matrix, matrix, vector, vector, vector, vector, vector, matrix)
    return jax.shard_map(
        body,
        mesh=mesh,
        in_specs=(rows, rows, *params),
        out_specs=(rows, rows, *params),
        check_vma=False,
    )
```
